256 devices in a mesh: col: 16 (over z, core), row: 16 (over x, y).
Axes of the slice: x: 4, y: 4, z: 8, core: 2. Of those that a mesh axis runs over, the one named last changes fastest.
Arguments:
- visibility: float32 [128, 2, 1024], P('row'), may hold values from -6 to 6
- baseline_uv: float32 [128, 2, 1024], P('row'), may hold values from 0 to 1024
- offsets: int32 [128, 2], P('row'), may hold values from 0 to 32767
- counts: int32 [128], P('row'), may hold values from 1 to 1024, 81920 in all
- taper_x: float32 [1024], replicated, may hold values from 0.1 to 1.9
- taper_y: float32 [1024], replicated, may hold values from 0.1 to 1.9
Outputs:
- image: float32 [2, 1024, 1024], P(None, 'col', 'row')
The draws below stay inside these ranges and needn't reach their ends.
Inputs may be any that keep to these rules, and one draw needn't show every extreme that they name: subgrid s has live visibilities in its first counts[s] slots; the other slots hold data that must be ignored.
All inputs are finite; a program needn't handle non-finite values. No bound on the sum of `counts` on one device may be relied on, other than what follows from the above.
Results may differ from the reference program's by a relative error of at most 0.0063.
Values may be sent and summed in bfloat16 or wider, within the bound.
A program may use at most 128 MiB of HBM per device.

```python
import math
import jax
import jax.numpy as jnp
import numpy as np
from jax import lax

SUBGRID = 1024
IMAGE = 32768
NVIS = 1024
NSUB = 128


def plant(drawn, rng, low, top_value):
    extent = drawn.shape
    spot = [jax.random.randint(jax.random.fold_in(rng, axis), (), 0, extent[axis]) for axis in range(len(extent))]
    drawn = drawn.at[tuple(spot)].set(low)
    longest = extent.index(max(extent))
    spot[longest] = (spot[longest] + 1) % extent[longest]
    return drawn.at[tuple(spot)].set(top_value)


def steps_of(rng, dims, cuts, low, largest):
    loudness, own = 1.0, jax.random.fold_in(rng, 6)
    for dim, shards_of in cuts:
        steps = jnp.exp(jax.random.uniform(jax.random.fold_in(own, dim), (shards_of,), jnp.float32, low / len(cuts), largest / len(cuts)))
        loudness = loudness * jnp.repeat(steps, dims[dim] // shards_of).reshape([-1 if axis == dim else 1 for axis in range(len(dims))])
    return loudness


def length_profile(number_of, total, reach, slope):
    weights = [(1 << 20) // math.isqrt(standing ** slope) + 1 for standing in range(2, number_of + 1)]
    surplus, holding = total - reach - (number_of - 1), [1] * (number_of - 1)
    while surplus > 0:
        movable = [i for i in range(number_of - 1) if holding[i] < reach]
        whole, budget = sum([weights[i] for i in movable]), surplus
        for i in movable:
            addition = min(reach - holding[i], max(1, budget * weights[i] // whole), surplus)
            holding[i] = holding[i] + addition
            surplus = surplus - addition
    return np.array([reach] + holding)


def uneven_parts(own_key, count, total, limit, skew):
    if count == 2:
        one = jax.random.randint(own_key, (), max(1, total - limit), min(limit, total - 1) + 1)
        return jnp.stack([one, total - one])
    lengths = jnp.asarray(length_profile(count, total, limit, skew), jnp.int32)
    couples = (count - 1) // 2
    donor, sink = lengths[1:1 + 2 * couples:2], lengths[2:2 + 2 * couples:2]
    room = jnp.minimum(donor - 1, limit - sink)
    moved = jax.random.randint(jax.random.fold_in(own_key, 1), (couples,), 0, 1 << 20) % (room + 1)
    lengths = lengths.at[1:1 + 2 * couples:2].set(donor - moved).at[2:2 + 2 * couples:2].set(sink + moved)
    return lengths[jax.random.permutation(jax.random.fold_in(own_key, 2), count)]


def centred(stream_key, shape, width, reach, split=(), held_as=jnp.bfloat16):
    array = jax.random.normal(stream_key, shape, jnp.float32) * width
    if len(split) > 0:
        array = steps_of(stream_key, shape, split, -0.22, 0.18) * array
    return jnp.clip(array, min=-reach, max=reach).astype(held_as)


def setup_inputs(seed: int = 0) -> dict:
    keys = jax.random.split(jax.random.key(seed), 7)
    visibility = centred(keys[0], (NSUB, 2, NVIS), 1.0, 6.0, ((0, 16),), jnp.float32)
    baseline_uv = jnp.clip(1024.0 * jax.random.uniform(keys[1], (NSUB, 2, NVIS), jnp.float32) ** steps_of(keys[1], (NSUB, 2, NVIS), ((0, 16),), -0.2, 0.2), 0.0, 1024.0)
    offsets = plant(jax.random.randint(keys[2], (NSUB, 2), 0, IMAGE), jax.random.fold_in(keys[2], 1), 0, IMAGE - 1).astype(jnp.int32)
    counts = uneven_parts(keys[3], NSUB, NSUB * NVIS * 5 // 8, NVIS, 1).astype(jnp.int32)
    taper_x = jnp.clip(1.0 + 0.18 * jax.random.normal(keys[4], (SUBGRID,), jnp.float32), 0.1, 1.9)
    taper_y = jnp.clip(1.0 + 0.18 * jax.random.normal(keys[5], (SUBGRID,), jnp.float32), 0.1, 1.9)
    return dict(visibility=visibility, baseline_uv=baseline_uv, offsets=offsets, counts=counts, taper_x=taper_x, taper_y=taper_y)


def sample_pixels(grid_side):
    position = jnp.arange(grid_side, dtype=jnp.int32)
    stride = IMAGE // grid_side - 1
    return jnp.mod(stride * position - IMAGE // 2, IMAGE)

def dft_tables(grid_side):
    position = jnp.arange(grid_side, dtype=jnp.int32)
    pixels = sample_pixels(grid_side)
    turn_count = jnp.mod(pixels[:, None] * position[None, :], IMAGE)
    angles = 2.0 * math.pi / IMAGE * turn_count.astype(jnp.float32)
    return (jnp.cos(angles).astype(jnp.bfloat16), jnp.sin(angles).astype(jnp.bfloat16))

def offset_phases(offset_col, grid_side):
    pixels = sample_pixels(grid_side)
    shifted = jnp.mod(offset_col.astype(jnp.int32), IMAGE)
    turn_count = jnp.mod(pixels[None, :] * shifted[:, None], IMAGE)
    angles = 2.0 * math.pi / IMAGE * turn_count.astype(jnp.float32)
    return (jnp.cos(angles), jnp.sin(angles))

def reference(visibility, baseline_uv, offsets, counts, taper_x, taper_y):
    table_re, table_im = dft_tables(SUBGRID)
    ucos, usin = offset_phases(offsets[:, 0], SUBGRID)
    vcos, vsin = offset_phases(offsets[:, 1], SUBGRID)
    position = jnp.arange(SUBGRID, dtype=jnp.float32)
    chirp_rate = math.pi / SUBGRID
    norm_scale = 4.0 / (SUBGRID * math.sqrt(NSUB * NVIS))

    def one_subgrid(running, inputs):
        vis_rows, uv_rows, live_count, cos_u, sin_u, cos_v, sin_v = inputs
        live_mask = (jnp.arange(NVIS, dtype=jnp.int32) < live_count).astype(jnp.float32)
        kernel_u = jnp.cos(chirp_rate * (position[None, :] - uv_rows[0][:, None]) ** 2).astype(jnp.bfloat16)
        kernel_v = jnp.cos(chirp_rate * (position[None, :] - uv_rows[1][:, None]) ** 2)
        weight_re = ((vis_rows[0] * live_mask)[:, None] * kernel_v).astype(jnp.bfloat16)
        weight_im = ((vis_rows[1] * live_mask)[:, None] * kernel_v).astype(jnp.bfloat16)
        grid_re = jnp.dot(kernel_u.T, weight_re, preferred_element_type=jnp.float32).astype(jnp.bfloat16)
        grid_im = jnp.dot(kernel_u.T, weight_im, preferred_element_type=jnp.float32).astype(jnp.bfloat16)
        real_raw = jnp.dot(table_re, grid_re, preferred_element_type=jnp.float32) - jnp.dot(table_im, grid_im, preferred_element_type=jnp.float32)
        imag_raw = jnp.dot(table_re, grid_im, preferred_element_type=jnp.float32) + jnp.dot(table_im, grid_re, preferred_element_type=jnp.float32)
        col_real = (taper_x[:, None] * (cos_u[:, None] * real_raw - sin_u[:, None] * imag_raw)).astype(jnp.bfloat16)
        col_imag = (taper_x[:, None] * (cos_u[:, None] * imag_raw + sin_u[:, None] * real_raw)).astype(jnp.bfloat16)
        row_real = jnp.dot(col_real, table_re.T, preferred_element_type=jnp.float32) - jnp.dot(col_imag, table_im.T, preferred_element_type=jnp.float32)
        row_imag = jnp.dot(col_real, table_im.T, preferred_element_type=jnp.float32) + jnp.dot(col_imag, table_re.T, preferred_element_type=jnp.float32)
        out_real = taper_y[None, :] * (cos_v[None, :] * row_real - sin_v[None, :] * row_imag)
        out_imag = taper_y[None, :] * (cos_v[None, :] * row_imag + sin_v[None, :] * row_real)
        return (running + norm_scale * jnp.stack([out_real, out_imag]), None)
    start = jnp.zeros((2, SUBGRID, SUBGRID), jnp.float32)
    image, _ = lax.scan(one_subgrid, start, (visibility, baseline_uv, counts, ucos, usin, vcos, vsin))
    return image
```

```python
import functools
import math

import jax
import jax.numpy as jnp
import numpy as np
from jax import lax
from jax.experimental import pallas as pl
from jax.experimental.pallas import tpu as pltpu
from jax.sharding import PartitionSpec as P

IMAGE = 32768
SIDE = 1024
HALF = SIDE // 2
STRIDE = IMAGE // SIDE - 1
OWN = 4
ROWS = 128
MESH = pl.DeviceIdType.MESH

COS_POLY = (
    0.9999999890588229,
    -19.73920449945383,
    64.93911745989081,
    -85.45013953079767,
    60.167630950263465,
    -25.967599245923743,
    6.52865815775625,
)


def cos_turns(turns):
    frac = turns - jnp.round(turns)
    square = frac * frac
    value = COS_POLY[6] * square + COS_POLY[5]
    for factor in COS_POLY[4::-1]:
        value = value * square + factor
    return value


def half_table():
    pixel = STRIDE * np.arange(SIDE, dtype=np.int64) - IMAGE // 2
    odd = 2 * np.arange(HALF, dtype=np.int64) + 1
    angle = (2.0 * np.pi / (2 * IMAGE)) * np.mod(pixel[:, None] * odd[None, :], 2 * IMAGE)
    return np.concatenate([np.cos(angle), np.sin(angle)], axis=1).astype(jnp.bfloat16)


def chains(coord, emit):
    row = lax.broadcasted_iota(jnp.int32, (32, 128), 0).astype(jnp.float32)
    here = jnp.broadcast_to(coord, (32, 128))
    near = row - here
    up_mult = -2.0 * cos_turns(near * (1.0 / 32.0))
    down_mult = -2.0 * cos_turns((row + here + 1.0) * (1.0 / 32.0))

    def up_at(block):
        dist = near + float(HALF + 32 * block)
        return cos_turns(dist * dist * (1.0 / (2 * SIDE)))

    def down_at(block):
        dist = (row + here) - float(HALF - 1 - 32 * block)
        return cos_turns(dist * dist * (1.0 / (2 * SIDE)))

    up = [up_at(7), up_at(8)]
    down = [down_at(7), down_at(8)]
    emit(7, up[0], down[0])
    emit(8, up[1], down[1])
    after_up, before_up = up[1], up[0]
    after_down, before_down = down[1], down[0]
    for block in range(9, 16):
        after_up, before_up = up_mult * after_up - before_up, after_up
        after_down, before_down = down_mult * after_down - before_down, after_down
        emit(block, after_up, after_down)
    after_up, before_up = up[0], up[1]
    after_down, before_down = down[0], down[1]
    for block in range(6, -1, -1):
        after_up, before_up = up_mult * after_up - before_up, after_up
        after_down, before_down = down_mult * after_down - before_down, after_down
        emit(block, after_up, after_down)


def kernel(
    visibility,
    baseline,
    offsets,
    counts,
    taper_x,
    taper_y,
    table_hbm,
    result,
    table,
    even,
    odd,
    upper,
    lower,
    weighted,
    weights,
    phases,
    phase_u,
    kept,
    to_partner,
    from_partner,
    blocks,
    slots,
    table_sem,
    pair_send,
    pair_recv,
    block_send,
    block_recv,
):
    col = lax.axis_index("col")
    row = lax.axis_index("row")
    core = lax.rem(col, 2)
    plane = col // 2
    partner = col + 1 - 2 * core
    here_x = row // 4
    here_y = lax.rem(row, 4)

    load_table = pltpu.make_async_copy(table_hbm, table, table_sem)
    load_table.start()

    barrier = pltpu.get_barrier_semaphore()
    pl.semaphore_signal(barrier, inc=1, device_id={"col": partner, "row": row}, device_id_type=MESH)
    for step in range(1, 16):
        other = lax.rem(row + step, 16)
        pl.semaphore_signal(barrier, inc=1, device_id={"col": col, "row": other}, device_id_type=MESH)

    pixel = STRIDE * lax.broadcasted_iota(jnp.int32, (8, SIDE), 1) - IMAGE // 2
    scale = 4.0 / (SIDE * math.sqrt(float(128 * SIDE)))
    parts = []
    for axis, taper, factor in ((0, taper_x, 1.0), (1, taper_y, scale)):
        shift = 2 * offsets[:, axis : axis + 1] + (SIDE - 1)
        turns = (pixel * shift) & (2 * IMAGE - 1)
        frac = turns.astype(jnp.float32) * (1.0 / (2 * IMAGE))
        size = jnp.broadcast_to(taper[...] * factor, (8, SIDE))
        parts.append(size * cos_turns(frac))
        parts.append(size * cos_turns(frac - 0.25))
    first = core == 0
    own_parts = [jnp.where(first, part[0:4], part[4:8]) for part in parts]
    square = jnp.concatenate(own_parts + [jnp.zeros((ROWS - 16, SIDE), jnp.float32)], axis=0)
    phases[...] = square.T

    own_first = pl.multiple_of(plane * ROWS + core * 64, 64)
    other_first = pl.multiple_of(plane * ROWS + (1 - core) * 64, 64)
    for near, place in ((0, own_first), (1, other_first)):
        some = phases[pl.ds(place, 64), :]
        for sub in range(OWN):
            for part in range(2):
                column = some[:, 4 * part + sub : 4 * part + sub + 1]
                phase_u[sub, part, near] = jnp.broadcast_to(column, (64, 128))

    load_table.wait()

    def one_subgrid(sub, carry):
        which = core * OWN + sub
        live = counts[which]

        def fill_u(block, inner):
            lanes = pl.ds(pl.multiple_of(block * 128, 128), 128)

            def emit(at, up, down):
                even[pl.ds(32 * at, 32), lanes] = (up + down).astype(jnp.bfloat16)
                odd[pl.ds(32 * at, 32), lanes] = (up - down).astype(jnp.bfloat16)

            chains(baseline[which, 0:1, lanes], emit)
            return inner

        lax.fori_loop(0, 8, fill_u, 0)

        def fill_v(block, inner):
            lanes = pl.ds(pl.multiple_of(block * 128, 128), 128)

            def emit(at, up, down):
                upper[pl.ds(32 * at, 32), lanes] = up.astype(jnp.bfloat16)
                lower[pl.ds(32 * at, 32), lanes] = down.astype(jnp.bfloat16)

            chains(baseline[which, 1:2, lanes], emit)
            return inner

        lax.fori_loop(0, 8, fill_v, 0)

        for near, place in ((0, own_first), (1, other_first)):
            cos_rows = table[pl.ds(place, 64), 0:HALF]
            sin_rows = table[pl.ds(place, 64), HALF:SIDE]
            for block in range(4):
                lanes = slice(256 * block, 256 * block + 256)
                real = jnp.dot(cos_rows, even[:, lanes], preferred_element_type=jnp.float32)
                imag = jnp.dot(sin_rows, odd[:, lanes], preferred_element_type=jnp.float32)
                mask = lax.broadcasted_iota(jnp.int32, (1, 256), 1) + 256 * block < live
                vis_re = jnp.where(mask, visibility[which, 0:1, lanes], 0.0)
                vis_im = jnp.where(mask, visibility[which, 1:2, lanes], 0.0)
                mid_re = real * vis_re - imag * vis_im
                mid_im = real * vis_im + imag * vis_re
                turn_re = jnp.concatenate([phase_u[sub, 0, near]] * 2, axis=1)
                turn_im = jnp.concatenate([phase_u[sub, 1, near]] * 2, axis=1)
                out_re = mid_re * turn_re - mid_im * turn_im
                out_im = mid_re * turn_im + mid_im * turn_re
                weighted[128 * near : 128 * near + 64, lanes] = out_re.astype(jnp.bfloat16)
                weighted[128 * near + 64 : 128 * near + 128, lanes] = out_im.astype(jnp.bfloat16)

        sign = jnp.where(lax.broadcasted_iota(jnp.int32, (128, 128), 1) < 64, -1.0, 1.0)

        def gather_k(tile, inner):
            at = pl.ds(pl.multiple_of(tile * 128, 128), 128)
            contract = (((1,), (1,)), ((), ()))
            plus = lax.dot_general(
                upper[at, :], weighted[...], contract, preferred_element_type=jnp.float32
            )
            minus = lax.dot_general(
                lower[at, :], weighted[...], contract, preferred_element_type=jnp.float32
            )
            weights[sub, at, :] = (plus + minus).astype(jnp.bfloat16)
            diff = plus - minus
            at_odd = pl.ds(pl.multiple_of(HALF + tile * 128, 128), 128)
            for near in range(2):
                turned = pltpu.roll(diff[:, 128 * near : 128 * near + 128], 64, 1) * sign
                weights[sub, at_odd, 128 * near : 128 * near + 128] = turned.astype(jnp.bfloat16)
            return inner

        lax.fori_loop(0, 4, gather_k, 0)
        return carry

    lax.fori_loop(0, OWN, one_subgrid, 0)

    sign_row = jnp.where(lax.broadcasted_iota(jnp.int32, (256, 128), 1) < 64, -1.0, 1.0)

    def pair_copy(step):
        return pltpu.make_async_remote_copy(
            src_ref=to_partner.at[step],
            dst_ref=from_partner.at[step],
            send_sem=pair_send.at[step],
            recv_sem=pair_recv.at[step],
            device_id={"col": partner, "row": row},
            device_id_type=MESH,
        )

    def block_copy(step, hop):
        to_x = lax.rem(here_x + 3 - step, 4)
        to_y = lax.rem(here_y + hop, 4)
        return pltpu.make_async_remote_copy(
            src_ref=blocks.at[step, hop],
            dst_ref=slots.at[step, hop],
            send_sem=block_send.at[step, hop],
            recv_sem=block_recv.at[step, hop],
            device_id={"col": col, "row": to_x * 4 + to_y},
            device_id_type=MESH,
        )

    def transform(step):
        to_x = lax.rem(here_x + 3 - step, 4)
        place = pl.ds(pl.multiple_of(to_x * 256, 256), 256)
        lhs = table[place, :]
        columns = phases[place, :]
        sums = [jnp.zeros((256, 128), jnp.float32)] * 2
        for sub in range(OWN):
            product = jnp.dot(lhs, weights[sub], preferred_element_type=jnp.float32)
            turn_re = jnp.broadcast_to(columns[:, 8 + sub : 9 + sub], (256, 128))
            turn_im = jnp.broadcast_to(columns[:, 12 + sub : 13 + sub], (256, 128)) * sign_row
            for near in range(2):
                part = product[:, 128 * near : 128 * near + 128]
                sums[near] = sums[near] + (part * turn_re + pltpu.roll(part, 64, 1) * turn_im)
        kept[step] = sums[0]
        to_partner[step] = sums[1].astype(jnp.bfloat16)

    def finish(step):
        pair_copy(step).wait_recv()
        both = kept[step] + from_partner[step].astype(jnp.float32)
        kept[step] = both
        for hop in range(4):
            to_y = lax.rem(here_y + hop, 4)
            if step == 3 and hop == 0:
                continue
            piece = kept[step, pl.ds(pl.multiple_of(to_y * 64, 64), 64), :]
            blocks[step, hop] = piece.astype(jnp.bfloat16)
            block_copy(step, hop).start()

    for step in range(4):
        transform(step)
        if step == 0:
            pl.semaphore_wait(barrier, 16)
        pair_copy(step).start()
        if step > 0:
            finish(step - 1)
    finish(3)

    total = kept[3, pl.ds(pl.multiple_of(here_y * 64, 64), 64), :]
    for step in range(4):
        for hop in range(4):
            if step == 3 and hop == 0:
                continue
            block_copy(step, hop).wait_recv()
            total = total + slots[step, hop].astype(jnp.float32)
    result[...] = total
    for step in range(4):
        pair_copy(step).wait_send()
        for hop in range(4):
            if step == 3 and hop == 0:
                continue
            block_copy(step, hop).wait_send()


def per_device(visibility, baseline, offsets, counts, taper_x, taper_y):
    vmem = pl.BlockSpec(memory_space=pltpu.VMEM)
    smem = pl.BlockSpec(memory_space=pltpu.SMEM)
    half = jnp.bfloat16
    full = jnp.float32
    total = pl.pallas_call(
        kernel,
        out_shape=jax.ShapeDtypeStruct((64, 128), full),
        in_specs=[vmem, vmem, vmem, smem, vmem, vmem, pl.BlockSpec(memory_space=pl.ANY)],
        out_specs=vmem,
        scratch_shapes=[
            pltpu.VMEM((SIDE, SIDE), half),
            pltpu.VMEM((HALF, SIDE), half),
            pltpu.VMEM((HALF, SIDE), half),
            pltpu.VMEM((HALF, SIDE), half),
            pltpu.VMEM((HALF, SIDE), half),
            pltpu.VMEM((2 * ROWS, SIDE), half),
            pltpu.VMEM((OWN, SIDE, 2 * ROWS), half),
            pltpu.VMEM((SIDE, 128), full),
            pltpu.VMEM((OWN, 2, 2, 64, 128), full),
            pltpu.VMEM((4, 256, 128), full),
            pltpu.VMEM((4, 256, 128), half),
            pltpu.VMEM((4, 256, 128), half),
            pltpu.VMEM((4, 4, 64, 128), half),
            pltpu.VMEM((4, 4, 64, 128), half),
            pltpu.SemaphoreType.DMA,
            pltpu.SemaphoreType.DMA((4,)),
            pltpu.SemaphoreType.DMA((4,)),
            pltpu.SemaphoreType.DMA((4, 4)),
            pltpu.SemaphoreType.DMA((4, 4)),
        ],
        compiler_params=pltpu.CompilerParams(
            collective_id=0, has_side_effects=True, vmem_limit_bytes=40 * 1024 * 1024
        ),
        name="facet_rows",
    )(
        visibility,
        baseline,
        offsets,
        counts,
        taper_x.reshape(1, SIDE),
        taper_y.reshape(1, SIDE),
        jnp.asarray(half_table()),
    )
    return total.T.reshape(2, 64, 64)


def solution(mesh):
    placed = (P("row", None, None), P("row", None, None), P("row", None), P("row"), P(), P())
    return jax.shard_map(
        per_device, mesh=mesh, in_specs=placed, out_specs=P(None, "col", "row"), check_vma=False
    )
```

```python
import functools
import math

import jax
import jax.numpy as jnp
import numpy as np
from jax import lax
from jax.experimental import pallas as pl
from jax.experimental.pallas import tpu as pltpu
from jax.sharding import PartitionSpec as P

IMAGE = 32768
SIDE = 1024
HALF = SIDE // 2
STRIDE = IMAGE // SIDE - 1
OWN = 4
ROWS = 128
MESH = pl.DeviceIdType.MESH

COS_POLY = (
    0.9999999890588229,
    -19.73920449945383,
    64.93911745989081,
    -85.45013953079767,
    60.167630950263465,
    -25.967599245923743,
    6.52865815775625,
)


def cos_turns(turns):
    frac = turns - jnp.round(turns)
    square = frac * frac
    value = COS_POLY[6] * square + COS_POLY[5]
    for factor in COS_POLY[4::-1]:
        value = value * square + factor
    return value


def half_table():
    pixel = STRIDE * np.arange(SIDE, dtype=np.int64) - IMAGE // 2
    odd = 2 * np.arange(HALF, dtype=np.int64) + 1
    angle = (2.0 * np.pi / (2 * IMAGE)) * np.mod(pixel[:, None] * odd[None, :], 2 * IMAGE)
    return np.concatenate([np.cos(angle), np.sin(angle)], axis=1).astype(jnp.bfloat16)


def chains(coord, turns, emit):
    row = lax.broadcasted_iota(jnp.int32, (32, 128), 0).astype(jnp.float32)
    near = row - jnp.broadcast_to(coord, (32, 128))
    small = jnp.broadcast_to(coord * (1.0 / 32.0), (8, 128))
    cos_here = jnp.concatenate([cos_turns(small)] * 4, axis=0)
    sin_here = jnp.concatenate([cos_turns(small - 0.25)] * 4, axis=0)
    multiplier = turns[0:32] * cos_here + turns[32:64] * sin_here

    def anchor(block):
        dist = near + float(32 * block)
        return cos_turns(dist * dist * (1.0 / (2 * SIDE)))

    flip = 7 - lax.broadcasted_iota(jnp.int32, (8, 128), 0)

    def reverse(block):
        pieces = [block[8 * i : 8 * i + 8] for i in range(3, -1, -1)]
        return jnp.concatenate([jnp.take_along_axis(p, flip, axis=0) for p in pieces], axis=0)

    below, above = anchor(15), anchor(16)
    starts = ((multiplier, below, above), tuple(map(reverse, (multiplier, above, below))))
    for part, (factor, before, now) in enumerate(starts):
        for block in range(16):
            emit(part, block, now)
            if block < 15:
                now, before = factor * now - before, now


def kernel(
    visibility_hbm,
    baseline_hbm,
    offsets_hbm,
    counts_hbm,
    taper_x_hbm,
    taper_y_hbm,
    table_hbm,
    result,
    visibility,
    baseline,
    offsets,
    counts,
    taper,
    table,
    own_table,
    turns,
    grid_u,
    grid_v,
    weighted,
    weights,
    phases,
    phase_u,
    kept,
    to_partner,
    from_partner,
    blocks,
    slots,
    load_sem,
    pair_send,
    pair_recv,
    block_send,
    block_recv,
):
    col = lax.axis_index("col")
    row = lax.axis_index("row")
    core = lax.rem(col, 2)
    plane = col // 2
    partner = col + 1 - 2 * core
    here_x = row // 4
    here_y = lax.rem(row, 4)

    own = pl.ds(core * OWN, OWN)
    loads = [
        pltpu.make_async_copy(baseline_hbm.at[own], baseline, load_sem.at[0]),
        pltpu.make_async_copy(offsets_hbm, offsets, load_sem.at[1]),
        pltpu.make_async_copy(taper_x_hbm, taper.at[0], load_sem.at[2]),
        pltpu.make_async_copy(taper_y_hbm, taper.at[1], load_sem.at[3]),
        pltpu.make_async_copy(counts_hbm, counts, load_sem.at[4]),
        pltpu.make_async_copy(visibility_hbm.at[own], visibility, load_sem.at[5]),
        pltpu.make_async_copy(table_hbm, table, load_sem.at[6]),
    ]
    for load in loads:
        load.start()

    barrier = pltpu.get_barrier_semaphore()
    pl.semaphore_signal(barrier, inc=1, device_id={"col": partner, "row": row}, device_id_type=MESH)
    for step in range(1, 16):
        other = lax.rem(row + step, 16)
        pl.semaphore_signal(barrier, inc=1, device_id={"col": col, "row": other}, device_id_type=MESH)

    circle = lax.broadcasted_iota(jnp.int32, (32, 128), 0).astype(jnp.float32) * (1.0 / 32.0)
    turns[0:32] = -2.0 * cos_turns(circle)
    turns[32:64] = -2.0 * cos_turns(circle - 0.25)

    def fill_u(sub, block):
        def emit(part, at, value):
            grid_u[block, HALF * part + 32 * at : HALF * part + 32 * at + 32] = value.astype(jnp.bfloat16)

        lanes = pl.ds(block * 128, 128) if isinstance(block, int) else pl.ds(pl.multiple_of(block * 128, 128), 128)
        chains(baseline[sub, 0:1, lanes], turns, emit)

    def fill_v(sub, block):
        def emit(part, at, value):
            first = 256 * (at // 4) + 128 * part + 32 * (at % 4)
            grid_v[block, first : first + 32] = value.astype(jnp.bfloat16)

        lanes = pl.ds(block * 128, 128) if isinstance(block, int) else pl.ds(pl.multiple_of(block * 128, 128), 128)
        chains(baseline[sub, 1:2, lanes], turns, emit)

    for load in loads[:4]:
        load.wait()

    def first_fill(block, inner):
        fill_u(0, block)
        return inner

    lax.fori_loop(0, 8, first_fill, 0)

    pixel = STRIDE * lax.broadcasted_iota(jnp.int32, (8, SIDE), 1) - IMAGE // 2
    subgrid = lax.broadcasted_iota(jnp.int32, (8, SIDE), 0)
    scale = 4.0 / (SIDE * math.sqrt(float(128 * SIDE)))
    parts = []
    for axis, factor in ((0, 1.0), (1, scale)):
        shift = jnp.zeros((8, SIDE), jnp.int32)
        for sub in range(OWN):
            shift = jnp.where(subgrid == sub, 2 * offsets[axis, core * OWN + sub] + (SIDE - 1), shift)
        frac = ((pixel * shift) & (2 * IMAGE - 1)).astype(jnp.float32) * (1.0 / (2 * IMAGE))
        size = jnp.broadcast_to(taper[axis] * factor, (8, SIDE))
        parts.append(size * cos_turns(frac))
        parts.append(size * cos_turns(frac - 0.25))
    square = jnp.concatenate(parts + [jnp.zeros((ROWS - 32, SIDE), jnp.float32)], axis=0)
    phases[...] = square.T

    for load in loads[4:]:
        load.wait()

    for near in range(2):
        place = pl.multiple_of(plane * ROWS + (core if near == 0 else 1 - core) * 64, 64)
        some = phases[pl.ds(place, 64), :]
        for sub in range(OWN):
            for part in range(2):
                column = some[:, 8 * part + sub : 8 * part + sub + 1]
                phase_u[sub, near, part] = jnp.broadcast_to(column, (64, 128))
        cos_rows = table[pl.ds(place, 64), 0:HALF]
        sin_rows = table[pl.ds(place, 64), HALF:SIDE]
        own_table[128 * near : 128 * near + 64, 0:HALF] = cos_rows
        own_table[128 * near : 128 * near + 64, HALF:SIDE] = cos_rows
        own_table[128 * near + 64 : 128 * near + 128, 0:HALF] = sin_rows
        own_table[128 * near + 64 : 128 * near + 128, HALF:SIDE] = -sin_rows

    slot = lax.broadcasted_iota(jnp.int32, (2, SIDE), 1)
    for sub in range(OWN):
        mask = slot < counts[core * OWN + sub]
        visibility[sub] = jnp.where(mask, visibility[sub], 0.0)

    def rows_of_image(sub, step):
        rhs = jnp.concatenate([grid_u[2 * step], grid_u[2 * step + 1]], axis=1)
        product = jnp.dot(own_table[...], rhs, preferred_element_type=jnp.float32)
        lanes = pl.ds(step * 256, 256)
        vis_re = visibility[sub, 0:1, lanes]
        vis_im = visibility[sub, 1:2, lanes]
        for near in range(2):
            real = product[128 * near : 128 * near + 64]
            imag = product[128 * near + 64 : 128 * near + 128]
            mid_re = real * vis_re - imag * vis_im
            mid_im = real * vis_im + imag * vis_re
            turn_re = jnp.concatenate([phase_u[sub, near, 0]] * 2, axis=1)
            turn_im = jnp.concatenate([phase_u[sub, near, 1]] * 2, axis=1)
            out_re = mid_re * turn_re - mid_im * turn_im
            out_im = mid_re * turn_im + mid_im * turn_re
            both = jnp.concatenate([out_re, out_im], axis=0).astype(jnp.bfloat16)
            weighted[near, lanes, :] = both.T

    sign = jnp.where(lax.broadcasted_iota(jnp.int32, (128, 128), 1) < 64, -1.0, 1.0)

    def columns_of_grid(sub, step):
        place = pl.ds(step * 256, 256)
        lhs = jnp.concatenate([grid_v[i, place, :] for i in range(8)], axis=1)
        rhs = jnp.concatenate([weighted[0], weighted[1]], axis=1)
        product = jnp.dot(lhs, rhs, preferred_element_type=jnp.float32)
        plus, minus = product[0:128], product[128:256]
        at = pl.ds(step * 128, 128)
        at_odd = pl.ds(HALF + step * 128, 128)
        total = (plus + minus).astype(jnp.bfloat16)
        diff = plus - minus
        for near in range(2):
            lanes = slice(128 * near, 128 * near + 128)
            weights[sub, near, at, :] = total[:, lanes]
            weights[sub, near, at_odd, :] = (pltpu.roll(diff[:, lanes], 64, 1) * sign).astype(jnp.bfloat16)

    def one_subgrid(sub, carry):
        def first_half(step, inner):
            rows_of_image(sub, step)
            fill_v(sub, 2 * step)
            fill_v(sub, 2 * step + 1)
            return inner

        def second_half(step, inner):
            columns_of_grid(sub, step)
            fill_u(jnp.minimum(sub + 1, OWN - 1), 2 * step)
            fill_u(jnp.minimum(sub + 1, OWN - 1), 2 * step + 1)
            return inner

        for step in range(4):
            first_half(step, 0)
        for step in range(4):
            second_half(step, 0)
        return carry

    lax.fori_loop(0, OWN, one_subgrid, 0)

    sign_row = jnp.where(lax.broadcasted_iota(jnp.int32, (256, 128), 1) < 64, -1.0, 1.0)

    def pair_copy(step):
        return pltpu.make_async_remote_copy(
            src_ref=to_partner.at[step],
            dst_ref=from_partner.at[step],
            send_sem=pair_send.at[step],
            recv_sem=pair_recv.at[step],
            device_id={"col": partner, "row": row},
            device_id_type=MESH,
        )

    def block_copy(step, hop):
        to_x = lax.rem(here_x + 3 - step, 4)
        to_y = lax.rem(here_y + hop, 4)
        return pltpu.make_async_remote_copy(
            src_ref=blocks.at[step, hop],
            dst_ref=slots.at[step, hop],
            send_sem=block_send.at[step, hop],
            recv_sem=block_recv.at[step, hop],
            device_id={"col": col, "row": to_x * 4 + to_y},
            device_id_type=MESH,
        )

    def transform(step):
        to_x = lax.rem(here_x + 3 - step, 4)
        place = pl.ds(pl.multiple_of(to_x * 256, 256), 256)
        lhs = table[place, :]
        columns = phases[place, :]
        sums = [jnp.zeros((256, 128), jnp.float32)] * 2
        for sub in range(OWN):
            rhs = jnp.concatenate([weights[sub, 0], weights[sub, 1]], axis=1)
            product = jnp.dot(lhs, rhs, preferred_element_type=jnp.float32)
            turn_re = jnp.broadcast_to(columns[:, 16 + sub : 17 + sub], (256, 128))
            turn_im = jnp.broadcast_to(columns[:, 24 + sub : 25 + sub], (256, 128)) * sign_row
            for near in range(2):
                part = product[:, 128 * near : 128 * near + 128]
                sums[near] = sums[near] + (part * turn_re + pltpu.roll(part, 64, 1) * turn_im)
        kept[step] = sums[0]
        to_partner[step] = sums[1].astype(jnp.bfloat16)

    def finish(step):
        pair_copy(step).wait_recv()
        both = kept[step] + from_partner[step].astype(jnp.float32)
        kept[step] = both
        for hop in range(4):
            to_y = lax.rem(here_y + hop, 4)
            if step == 3 and hop == 0:
                continue
            piece = kept[step, pl.ds(pl.multiple_of(to_y * 64, 64), 64), :]
            blocks[step, hop] = piece.astype(jnp.bfloat16)
            block_copy(step, hop).start()

    for step in range(4):
        transform(step)
        if step == 0:
            pl.semaphore_wait(barrier, 16)
        pair_copy(step).start()
        if step > 0:
            finish(step - 1)
    finish(3)

    total = kept[3, pl.ds(pl.multiple_of(here_y * 64, 64), 64), :]
    for step in range(4):
        for hop in range(4):
            if step == 3 and hop == 0:
                continue
            block_copy(step, hop).wait_recv()
            total = total + slots[step, hop].astype(jnp.float32)
    result[...] = total
    for step in range(4):
        pair_copy(step).wait_send()
        for hop in range(4):
            if step == 3 and hop == 0:
                continue
            block_copy(step, hop).wait_send()


def per_device(visibility, baseline, offsets, counts, taper_x, taper_y):
    hbm = pl.BlockSpec(memory_space=pltpu.HBM)
    half = jnp.bfloat16
    full = jnp.float32
    total = pl.pallas_call(
        kernel,
        out_shape=jax.ShapeDtypeStruct((64, 128), full),
        in_specs=[hbm] * 7,
        out_specs=pl.BlockSpec(memory_space=pltpu.VMEM),
        scratch_shapes=[
            pltpu.VMEM((OWN, 2, SIDE), full),
            pltpu.VMEM((OWN, 2, SIDE), full),
            pltpu.SMEM((2, 8), jnp.int32),
            pltpu.SMEM((8,), jnp.int32),
            pltpu.VMEM((2, 1, SIDE), full),
            pltpu.VMEM((SIDE, SIDE), half),
            pltpu.VMEM((2 * ROWS, SIDE), half),
            pltpu.VMEM((64, 128), full),
            pltpu.VMEM((8, SIDE, 128), half),
            pltpu.VMEM((8, SIDE, 128), half),
            pltpu.VMEM((2, SIDE, 128), half),
            pltpu.VMEM((OWN, 2, SIDE, 128), half),
            pltpu.VMEM((SIDE, 128), full),
            pltpu.VMEM((OWN, 2, 2, 64, 128), full),
            pltpu.VMEM((4, 256, 128), full),
            pltpu.VMEM((4, 256, 128), half),
            pltpu.VMEM((4, 256, 128), half),
            pltpu.VMEM((4, 4, 64, 128), half),
            pltpu.VMEM((4, 4, 64, 128), half),
            pltpu.SemaphoreType.DMA((7,)),
            pltpu.SemaphoreType.DMA((4,)),
            pltpu.SemaphoreType.DMA((4,)),
            pltpu.SemaphoreType.DMA((4, 4)),
            pltpu.SemaphoreType.DMA((4, 4)),
        ],
        compiler_params=pltpu.CompilerParams(
            collective_id=0, has_side_effects=True, vmem_limit_bytes=67043328
        ),
        name="facet_rows",
    )(
        visibility,
        baseline,
        offsets.T,
        counts,
        taper_x.reshape(1, SIDE),
        taper_y.reshape(1, SIDE),
        jnp.asarray(half_table()),
    )
    return total.T.reshape(2, 64, 64)


def solution(mesh):
    placed = (P("row", None, None), P("row", None, None), P("row", None), P("row"), P(), P())
    return jax.shard_map(
        per_device, mesh=mesh, in_specs=placed, out_specs=P(None, "col", "row"), check_vma=False
    )
```

```python
import functools
import math

import jax
import jax.numpy as jnp
import numpy as np
from jax import lax
from jax.experimental import pallas as pl
from jax.experimental.pallas import tpu as pltpu
from jax.sharding import PartitionSpec as P

IMAGE = 32768
SIDE = 1024
HALF = SIDE // 2
STRIDE = IMAGE // SIDE - 1
OWN = 4
ROWS = 128
MESH = pl.DeviceIdType.MESH

COS_POLY = (
    0.9999999890588229,
    -19.73920449945383,
    64.93911745989081,
    -85.45013953079767,
    60.167630950263465,
    -25.967599245923743,
    6.52865815775625,
)


def cos_turns(turns):
    frac = turns - jnp.round(turns)
    square = frac * frac
    value = COS_POLY[6] * square + COS_POLY[5]
    for factor in COS_POLY[4::-1]:
        value = value * square + factor
    return value


def half_table():
    pixel = STRIDE * np.arange(SIDE, dtype=np.int64) - IMAGE // 2
    odd = 2 * np.arange(HALF, dtype=np.int64) + 1
    angle = (2.0 * np.pi / (2 * IMAGE)) * np.mod(pixel[:, None] * odd[None, :], 2 * IMAGE)
    return np.concatenate([np.cos(angle), np.sin(angle)], axis=1).astype(jnp.bfloat16)


def chains(coord, cos_here, sin_here, turns, emit):
    row = lax.broadcasted_iota(jnp.int32, (32, 128), 0).astype(jnp.float32)
    near = row - jnp.broadcast_to(coord, (32, 128))
    multiplier = turns[0:32] * cos_here + turns[32:64] * sin_here

    def anchor(block):
        dist = near + float(32 * block)
        return cos_turns(dist * dist * (1.0 / (2 * SIDE)))

    flip = 7 - lax.broadcasted_iota(jnp.int32, (8, 128), 0)

    def reverse(block):
        pieces = [block[8 * i : 8 * i + 8] for i in range(3, -1, -1)]
        return jnp.concatenate([jnp.take_along_axis(p, flip, axis=0) for p in pieces], axis=0)

    below, above = anchor(15), anchor(16)
    starts = ((multiplier, below, above), tuple(map(reverse, (multiplier, above, below))))
    for part, (factor, before, now) in enumerate(starts):
        for block in range(16):
            emit(part, block, now)
            if block < 15:
                now, before = factor * now - before, now


def kernel(
    visibility_hbm,
    baseline_hbm,
    offsets_hbm,
    counts_hbm,
    taper_x_hbm,
    taper_y_hbm,
    table_hbm,
    result,
    visibility,
    baseline,
    offsets,
    counts,
    taper,
    table,
    own_table,
    turns,
    coords,
    grid_u,
    grid_v,
    weighted,
    weights,
    phases,
    phase_u,
    phase_v,
    kept,
    to_partner,
    from_partner,
    blocks,
    slots,
    load_sem,
    pair_send,
    pair_recv,
    block_send,
    block_recv,
):
    col = lax.axis_index("col")
    row = lax.axis_index("row")
    core = lax.rem(col, 2)
    plane = col // 2
    partner = col + 1 - 2 * core
    here_x = row // 4
    here_y = lax.rem(row, 4)

    own = pl.ds(core * OWN, OWN)
    loads = [
        pltpu.make_async_copy(baseline_hbm.at[own], baseline, load_sem.at[0]),
        pltpu.make_async_copy(offsets_hbm, offsets, load_sem.at[1]),
        pltpu.make_async_copy(taper_x_hbm, taper.at[0], load_sem.at[2]),
        pltpu.make_async_copy(taper_y_hbm, taper.at[1], load_sem.at[3]),
        pltpu.make_async_copy(counts_hbm, counts, load_sem.at[4]),
        pltpu.make_async_copy(visibility_hbm.at[own], visibility, load_sem.at[5]),
        pltpu.make_async_copy(table_hbm, table, load_sem.at[6]),
    ]
    for load in loads:
        load.start()

    barrier = pltpu.get_barrier_semaphore()
    pl.semaphore_signal(barrier, inc=1, device_id={"col": partner, "row": row}, device_id_type=MESH)
    for step in range(1, 16):
        other = lax.rem(row + step, 16)
        pl.semaphore_signal(barrier, inc=1, device_id={"col": col, "row": other}, device_id_type=MESH)

    circle = lax.broadcasted_iota(jnp.int32, (32, 128), 0).astype(jnp.float32) * (1.0 / 32.0)
    turns[0:32] = -2.0 * cos_turns(circle)
    turns[32:64] = -2.0 * cos_turns(circle - 0.25)

    def fill_u(sub, block):
        def emit(part, at, value):
            grid_u[block, HALF * part + 32 * at : HALF * part + 32 * at + 32] = value.astype(jnp.bfloat16)

        lanes = pl.ds(block * 128, 128) if isinstance(block, int) else pl.ds(pl.multiple_of(block * 128, 128), 128)
        at = 2 * sub
        chains(coords[at : at + 1, lanes], coords[8 + at : 9 + at, lanes], coords[16 + at : 17 + at, lanes], turns, emit)

    def fill_v(sub, block):
        def emit(part, at, value):
            first = 256 * (at // 4) + 128 * part + 32 * (at % 4)
            grid_v[block, first : first + 32] = value.astype(jnp.bfloat16)

        lanes = pl.ds(block * 128, 128) if isinstance(block, int) else pl.ds(pl.multiple_of(block * 128, 128), 128)
        at = 2 * sub + 1
        chains(coords[at : at + 1, lanes], coords[8 + at : 9 + at, lanes], coords[16 + at : 17 + at, lanes], turns, emit)

    loads[0].wait()
    for sub in range(OWN):
        coords[2 * sub : 2 * sub + 2] = baseline[sub]
    small = coords[0:8] * (1.0 / 32.0)
    coords[8:16] = cos_turns(small)
    coords[16:24] = cos_turns(small - 0.25)

    def first_fill(block, inner):
        fill_u(0, block)
        return inner

    lax.fori_loop(0, 8, first_fill, 0)

    for load in loads[1:]:
        load.wait()

    pixel = STRIDE * lax.broadcasted_iota(jnp.int32, (8, SIDE), 1) - IMAGE // 2
    subgrid = lax.broadcasted_iota(jnp.int32, (8, SIDE), 0)
    scale = 4.0 / (SIDE * math.sqrt(float(128 * SIDE)))
    parts = []
    for axis, factor in ((0, 1.0), (1, scale)):
        shift = jnp.zeros((8, SIDE), jnp.int32)
        for sub in range(OWN):
            shift = jnp.where(subgrid == sub, 2 * offsets[axis, core * OWN + sub] + (SIDE - 1), shift)
        frac = ((pixel * shift) & (2 * IMAGE - 1)).astype(jnp.float32) * (1.0 / (2 * IMAGE))
        size = jnp.broadcast_to(taper[axis] * factor, (8, SIDE))
        parts.append(size * cos_turns(frac))
        parts.append(size * cos_turns(frac - 0.25))
    for part in range(2):
        chips = parts[part][:, 0:128]
        for other in range(1, 8):
            chips = jnp.where(plane == other, parts[part][:, 128 * other : 128 * other + 128], chips)
        phase_u[part] = chips
    square = jnp.concatenate(parts[2:4] + [jnp.zeros((ROWS - 16, SIDE), jnp.float32)], axis=0)
    phases[...] = square.T

    def spread(number):
        sub, part, quarter = number // 8, number // 4 % 2, number % 4
        place = slice(256 * quarter, 256 * quarter + 256)
        column = phases[place, 8 * part + sub : 8 * part + sub + 1]
        phase_v[sub, part, place] = jnp.broadcast_to(column, (256, 128))

    place = pl.ds(pl.multiple_of(plane * ROWS, ROWS), ROWS)
    cos_rows = table[place, 0:HALF]
    sin_rows = table[place, HALF:SIDE]
    own_table[0:ROWS, 0:HALF] = cos_rows
    own_table[0:ROWS, HALF:SIDE] = cos_rows
    own_table[ROWS : 2 * ROWS, 0:HALF] = sin_rows
    own_table[ROWS : 2 * ROWS, HALF:SIDE] = -sin_rows

    slot = lax.broadcasted_iota(jnp.int32, (2, SIDE), 1)
    for sub in range(OWN):
        mask = slot < counts[core * OWN + sub]
        visibility[sub] = jnp.where(mask, visibility[sub], 0.0)

    def rows_of_image(sub, step):
        rhs = jnp.concatenate([grid_u[2 * step], grid_u[2 * step + 1]], axis=1)
        product = jnp.dot(own_table[...], rhs, preferred_element_type=jnp.float32)
        lanes = pl.ds(step * 256, 256)
        vis_re = visibility[sub, 0:1, lanes]
        vis_im = visibility[sub, 1:2, lanes]
        real, imag = product[0:ROWS], product[ROWS : 2 * ROWS]
        weighted[0, lanes, :] = (real * vis_re - imag * vis_im).astype(jnp.bfloat16).T
        weighted[1, lanes, :] = (real * vis_im + imag * vis_re).astype(jnp.bfloat16).T

    def columns_of_grid(sub, step):
        place = pl.ds(step * 256, 256)
        lhs = jnp.concatenate([grid_v[i, place, :] for i in range(8)], axis=1)
        rhs = jnp.concatenate([weighted[0], weighted[1]], axis=1)
        product = jnp.dot(lhs, rhs, preferred_element_type=jnp.float32)
        plus, minus = product[0:128], product[128:256]
        at = pl.ds(step * 128, 128)
        at_odd = pl.ds(HALF + step * 128, 128)
        weights[sub, 0, at, :] = (plus[:, 0:128] + minus[:, 0:128]).astype(jnp.bfloat16)
        weights[sub, 1, at, :] = (plus[:, 128:256] + minus[:, 128:256]).astype(jnp.bfloat16)
        weights[sub, 0, at_odd, :] = (minus[:, 128:256] - plus[:, 128:256]).astype(jnp.bfloat16)
        weights[sub, 1, at_odd, :] = (plus[:, 0:128] - minus[:, 0:128]).astype(jnp.bfloat16)

    for sub in range(OWN):
        for step in range(4):
            rows_of_image(sub, step)
            fill_v(sub, 2 * step)
            fill_v(sub, 2 * step + 1)
            spread(8 * sub + step)
        for step in range(4):
            columns_of_grid(sub, step)
            spread(8 * sub + 4 + step)
            if sub + 1 < OWN:
                fill_u(sub + 1, 2 * step)
                fill_u(sub + 1, 2 * step + 1)

    low_lanes = lax.broadcasted_iota(jnp.int32, (256, 128), 1) < 64

    def pair_copy(step):
        return pltpu.make_async_remote_copy(
            src_ref=to_partner.at[step],
            dst_ref=from_partner.at[step],
            send_sem=pair_send.at[step],
            recv_sem=pair_recv.at[step],
            device_id={"col": partner, "row": row},
            device_id_type=MESH,
        )

    def block_copy(step, hop):
        to_x = lax.rem(here_x + 3 - step, 4)
        to_y = lax.rem(here_y + hop, 4)
        return pltpu.make_async_remote_copy(
            src_ref=blocks.at[step, hop],
            dst_ref=slots.at[step, hop],
            send_sem=block_send.at[step, hop],
            recv_sem=block_recv.at[step, hop],
            device_id={"col": col, "row": to_x * 4 + to_y},
            device_id_type=MESH,
        )

    def transform(step):
        to_x = lax.rem(here_x + 3 - step, 4)
        place = pl.ds(pl.multiple_of(to_x * 256, 256), 256)
        lhs = table[place, :]
        sum_re = jnp.zeros((256, 128), jnp.float32)
        sum_im = jnp.zeros((256, 128), jnp.float32)
        for sub in range(OWN):
            rhs = jnp.concatenate([weights[sub, 0], weights[sub, 1]], axis=1)
            product = jnp.dot(lhs, rhs, preferred_element_type=jnp.float32)
            real, imag = product[:, 0:128], product[:, 128:256]
            row_re, row_im = phase_u[0, sub : sub + 1], phase_u[1, sub : sub + 1]
            mid_re = real * row_re - imag * row_im
            mid_im = real * row_im + imag * row_re
            turn_re, turn_im = phase_v[sub, 0, place], phase_v[sub, 1, place]
            sum_re = sum_re + (mid_re * turn_re - mid_im * turn_im)
            sum_im = sum_im + (mid_re * turn_im + mid_im * turn_re)
        first = jnp.where(low_lanes, sum_re, pltpu.roll(sum_im, 64, 1))
        second = jnp.where(low_lanes, pltpu.roll(sum_re, 64, 1), sum_im)
        kept[step] = jnp.where(core == 0, first, second)
        to_partner[step] = jnp.where(core == 0, second, first).astype(jnp.bfloat16)

    def finish(step):
        pair_copy(step).wait_recv()
        both = kept[step] + from_partner[step].astype(jnp.float32)
        kept[step] = both
        for hop in range(4):
            to_y = lax.rem(here_y + hop, 4)
            if step == 3 and hop == 0:
                continue
            piece = kept[step, pl.ds(pl.multiple_of(to_y * 64, 64), 64), :]
            blocks[step, hop] = piece.astype(jnp.bfloat16)
            block_copy(step, hop).start()

    for step in range(4):
        transform(step)
        if step == 0:
            pl.semaphore_wait(barrier, 16)
        pair_copy(step).start()
        if step > 1:
            finish(step - 2)
    finish(2)
    finish(3)

    total = kept[3, pl.ds(pl.multiple_of(here_y * 64, 64), 64), :]
    for step in range(4):
        for hop in range(4):
            if step == 3 and hop == 0:
                continue
            block_copy(step, hop).wait_recv()
            total = total + slots[step, hop].astype(jnp.float32)
    result[...] = total
    for step in range(4):
        pair_copy(step).wait_send()
        for hop in range(4):
            if step == 3 and hop == 0:
                continue
            block_copy(step, hop).wait_send()


def per_device(visibility, baseline, offsets, counts, taper_x, taper_y):
    hbm = pl.BlockSpec(memory_space=pltpu.HBM)
    half = jnp.bfloat16
    full = jnp.float32
    total = pl.pallas_call(
        kernel,
        out_shape=jax.ShapeDtypeStruct((64, 128), full),
        in_specs=[hbm] * 7,
        out_specs=pl.BlockSpec(memory_space=pltpu.VMEM),
        scratch_shapes=[
            pltpu.VMEM((OWN, 2, SIDE), full),
            pltpu.VMEM((OWN, 2, SIDE), full),
            pltpu.SMEM((2, 8), jnp.int32),
            pltpu.SMEM((8,), jnp.int32),
            pltpu.VMEM((2, 1, SIDE), full),
            pltpu.VMEM((SIDE, SIDE), half),
            pltpu.VMEM((2 * ROWS, SIDE), half),
            pltpu.VMEM((64, 128), full),
            pltpu.VMEM((24, SIDE), full),
            pltpu.VMEM((8, SIDE, 128), half),
            pltpu.VMEM((8, SIDE, 128), half),
            pltpu.VMEM((2, SIDE, 128), half),
            pltpu.VMEM((OWN, 2, SIDE, 128), half),
            pltpu.VMEM((SIDE, 128), full),
            pltpu.VMEM((2, 8, 128), full),
            pltpu.VMEM((OWN, 2, SIDE, 128), full),
            pltpu.VMEM((4, 256, 128), full),
            pltpu.VMEM((4, 256, 128), half),
            pltpu.VMEM((4, 256, 128), half),
            pltpu.VMEM((4, 4, 64, 128), half),
            pltpu.VMEM((4, 4, 64, 128), half),
            pltpu.SemaphoreType.DMA((7,)),
            pltpu.SemaphoreType.DMA((4,)),
            pltpu.SemaphoreType.DMA((4,)),
            pltpu.SemaphoreType.DMA((4, 4)),
            pltpu.SemaphoreType.DMA((4, 4)),
        ],
        compiler_params=pltpu.CompilerParams(
            collective_id=0, has_side_effects=True, vmem_limit_bytes=67043328
        ),
        name="facet_rows",
    )(
        visibility,
        baseline,
        offsets.T,
        counts,
        taper_x.reshape(1, SIDE),
        taper_y.reshape(1, SIDE),
        jnp.asarray(half_table()),
    )
    return total.T.reshape(2, 64, 64)


def solution(mesh):
    placed = (P("row", None, None), P("row", None, None), P("row", None), P("row"), P(), P())
    return jax.shard_map(
        per_device, mesh=mesh, in_specs=placed, out_specs=P(None, "col", "row"), check_vma=False
    )
```

```python
import functools
import math

import jax
import jax.numpy as jnp
import numpy as np
from jax import lax
from jax.experimental import pallas as pl
from jax.experimental.pallas import tpu as pltpu
from jax.sharding import PartitionSpec as P

IMAGE = 32768
SIDE = 1024
HALF = SIDE // 2
STRIDE = IMAGE // SIDE - 1
OWN = 4
ORDER = (2, 3, 1, 0)
ROWS = 128
MESH = pl.DeviceIdType.MESH

COS_POLY = (
    0.9999999890588229,
    -19.73920449945383,
    64.93911745989081,
    -85.45013953079767,
    60.167630950263465,
    -25.967599245923743,
    6.52865815775625,
)


def cos_turns(turns):
    frac = turns - jnp.round(turns)
    square = frac * frac
    value = COS_POLY[6] * square + COS_POLY[5]
    for factor in COS_POLY[4::-1]:
        value = value * square + factor
    return value


def half_table():
    pixel = STRIDE * np.arange(SIDE, dtype=np.int64) - IMAGE // 2
    odd = 2 * np.arange(HALF, dtype=np.int64) + 1
    angle = (2.0 * np.pi / (2 * IMAGE)) * np.mod(pixel[:, None] * odd[None, :], 2 * IMAGE)
    return np.concatenate([np.cos(angle), np.sin(angle)], axis=1).astype(jnp.bfloat16)


def chains(coord, cos_here, sin_here, turns, emit):
    row = lax.broadcasted_iota(jnp.int32, (32, 128), 0).astype(jnp.float32)
    near = row - jnp.broadcast_to(coord, (32, 128))
    multiplier = turns[0:32] * cos_here + turns[32:64] * sin_here

    def anchor(block):
        dist = near + float(32 * block)
        return cos_turns(dist * dist * (1.0 / (2 * SIDE)))

    flip = 7 - lax.broadcasted_iota(jnp.int32, (8, 128), 0)

    def reverse(block):
        pieces = [block[8 * i : 8 * i + 8] for i in range(3, -1, -1)]
        return jnp.concatenate([jnp.take_along_axis(p, flip, axis=0) for p in pieces], axis=0)

    below, above = anchor(15), anchor(16)
    starts = ((multiplier, below, above), tuple(map(reverse, (multiplier, above, below))))
    for part, (factor, before, now) in enumerate(starts):
        for block in range(16):
            emit(part, block, now)
            if block < 15:
                now, before = factor * now - before, now


def kernel(
    visibility_hbm,
    baseline_hbm,
    offsets_hbm,
    counts_hbm,
    taper_x_hbm,
    taper_y_hbm,
    table_hbm,
    result,
    visibility,
    baseline,
    offsets,
    counts,
    taper,
    table,
    own_table,
    turns,
    coords,
    grid_u,
    grid_v,
    weighted,
    weights,
    phases,
    phase_u,
    phase_v,
    kept,
    blocks,
    slots,
    load_sem,
    block_send,
    block_recv,
):
    col = lax.axis_index("col")
    row = lax.axis_index("row")
    core = lax.rem(col, 2)
    plane = col // 2
    partner = col + 1 - 2 * core
    here_x = row // 4
    here_y = lax.rem(row, 4)

    own = pl.ds(core * OWN, OWN)
    loads = [
        pltpu.make_async_copy(baseline_hbm.at[own], baseline, load_sem.at[0]),
        pltpu.make_async_copy(offsets_hbm, offsets, load_sem.at[1]),
        pltpu.make_async_copy(taper_x_hbm, taper.at[0], load_sem.at[2]),
        pltpu.make_async_copy(taper_y_hbm, taper.at[1], load_sem.at[3]),
        pltpu.make_async_copy(counts_hbm, counts, load_sem.at[4]),
        pltpu.make_async_copy(visibility_hbm.at[own], visibility, load_sem.at[5]),
        pltpu.make_async_copy(table_hbm, table, load_sem.at[6]),
    ]
    for load in loads:
        load.start()

    barrier = pltpu.get_barrier_semaphore()
    pl.semaphore_signal(barrier, inc=1, device_id={"col": partner, "row": row}, device_id_type=MESH)
    for step in range(1, 16):
        other = lax.rem(row + step, 16)
        for near in (col, partner):
            pl.semaphore_signal(barrier, inc=1, device_id={"col": near, "row": other}, device_id_type=MESH)

    circle = lax.broadcasted_iota(jnp.int32, (32, 128), 0).astype(jnp.float32) * (1.0 / 32.0)
    turns[0:32] = -2.0 * cos_turns(circle)
    turns[32:64] = -2.0 * cos_turns(circle - 0.25)

    def fill_u(sub, block):
        def emit(part, at, value):
            grid_u[block, HALF * part + 32 * at : HALF * part + 32 * at + 32] = value.astype(jnp.bfloat16)

        lanes = pl.ds(block * 128, 128) if isinstance(block, int) else pl.ds(pl.multiple_of(block * 128, 128), 128)
        at = 2 * sub
        chains(coords[at : at + 1, lanes], coords[8 + at : 9 + at, lanes], coords[16 + at : 17 + at, lanes], turns, emit)

    def fill_v(sub, block):
        def emit(part, at, value):
            first = 256 * (at // 4) + 128 * part + 32 * (at % 4)
            grid_v[block, first : first + 32] = value.astype(jnp.bfloat16)

        lanes = pl.ds(block * 128, 128) if isinstance(block, int) else pl.ds(pl.multiple_of(block * 128, 128), 128)
        at = 2 * sub + 1
        chains(coords[at : at + 1, lanes], coords[8 + at : 9 + at, lanes], coords[16 + at : 17 + at, lanes], turns, emit)

    loads[0].wait()
    for sub in range(OWN):
        coords[2 * sub : 2 * sub + 2] = baseline[sub]
    small = coords[0:8] * (1.0 / 32.0)
    coords[8:16] = cos_turns(small)
    coords[16:24] = cos_turns(small - 0.25)

    def first_fill(block, inner):
        fill_u(0, block)
        return inner

    lax.fori_loop(0, 8, first_fill, 0)

    for load in loads[1:]:
        load.wait()

    pixel = STRIDE * lax.broadcasted_iota(jnp.int32, (8, SIDE), 1) - IMAGE // 2
    subgrid = lax.broadcasted_iota(jnp.int32, (8, SIDE), 0)
    scale = 4.0 / (SIDE * math.sqrt(float(128 * SIDE)))
    parts = []
    for axis, factor in ((0, 1.0), (1, scale)):
        shift = jnp.zeros((8, SIDE), jnp.int32)
        for sub in range(OWN):
            shift = jnp.where(subgrid == sub, 2 * offsets[axis, core * OWN + sub] + (SIDE - 1), shift)
        frac = ((pixel * shift) & (2 * IMAGE - 1)).astype(jnp.float32) * (1.0 / (2 * IMAGE))
        size = jnp.broadcast_to(taper[axis] * factor, (8, SIDE))
        parts.append(size * cos_turns(frac))
        parts.append(size * cos_turns(frac - 0.25))
    for part in range(2):
        chips = parts[part][:, 0:128]
        for other in range(1, 8):
            chips = jnp.where(plane == other, parts[part][:, 128 * other : 128 * other + 128], chips)
        phase_u[part] = chips
    square = jnp.concatenate(parts[2:4] + [jnp.zeros((ROWS - 16, SIDE), jnp.float32)], axis=0)
    phases[...] = square.T

    def spread(number):
        sub, part, quarter = number // 8, number // 4 % 2, number % 4
        place = slice(256 * quarter, 256 * quarter + 256)
        column = phases[place, 8 * part + sub : 8 * part + sub + 1]
        phase_v[sub, part, place] = jnp.broadcast_to(column, (256, 128))

    place = pl.ds(pl.multiple_of(plane * ROWS, ROWS), ROWS)
    cos_rows = table[place, 0:HALF]
    sin_rows = table[place, HALF:SIDE]
    own_table[0:ROWS, 0:HALF] = cos_rows
    own_table[0:ROWS, HALF:SIDE] = cos_rows
    own_table[ROWS : 2 * ROWS, 0:HALF] = sin_rows
    own_table[ROWS : 2 * ROWS, HALF:SIDE] = -sin_rows

    slot = lax.broadcasted_iota(jnp.int32, (2, SIDE), 1)
    for sub in range(OWN):
        mask = slot < counts[core * OWN + sub]
        visibility[sub] = jnp.where(mask, visibility[sub], 0.0)

    def rows_of_image(sub, step):
        rhs = jnp.concatenate([grid_u[2 * step], grid_u[2 * step + 1]], axis=1)
        product = jnp.dot(own_table[...], rhs, preferred_element_type=jnp.float32)
        lanes = pl.ds(step * 256, 256)
        vis_re = visibility[sub, 0:1, lanes]
        vis_im = visibility[sub, 1:2, lanes]
        real, imag = product[0:ROWS], product[ROWS : 2 * ROWS]
        weighted[0, lanes, :] = (real * vis_re - imag * vis_im).astype(jnp.bfloat16).T
        weighted[1, lanes, :] = (real * vis_im + imag * vis_re).astype(jnp.bfloat16).T

    def columns_of_grid(sub, step):
        place = pl.ds(step * 256, 256)
        lhs = jnp.concatenate([grid_v[i, place, :] for i in range(8)], axis=1)
        rhs = jnp.concatenate([weighted[0], weighted[1]], axis=1)
        product = jnp.dot(lhs, rhs, preferred_element_type=jnp.float32)
        plus, minus = product[0:128], product[128:256]
        at = pl.ds(step * 128, 128)
        at_odd = pl.ds(HALF + step * 128, 128)
        weights[sub, 0, at, :] = (plus[:, 0:128] + minus[:, 0:128]).astype(jnp.bfloat16)
        weights[sub, 1, at, :] = (plus[:, 128:256] + minus[:, 128:256]).astype(jnp.bfloat16)
        weights[sub, 0, at_odd, :] = (minus[:, 128:256] - plus[:, 128:256]).astype(jnp.bfloat16)
        weights[sub, 1, at_odd, :] = (plus[:, 0:128] - minus[:, 0:128]).astype(jnp.bfloat16)

    for sub in range(OWN):
        for step in range(4):
            rows_of_image(sub, step)
            fill_v(sub, 2 * step)
            fill_v(sub, 2 * step + 1)
            spread(8 * sub + step)
        for step in range(4):
            columns_of_grid(sub, step)
            spread(8 * sub + 4 + step)
            if sub + 1 < OWN:
                fill_u(sub + 1, 2 * step)
                fill_u(sub + 1, 2 * step + 1)

    low_lanes = lax.broadcasted_iota(jnp.int32, (256, 128), 1) < 64

    def block_copy(step, hop, side):
        to_x = lax.rem(here_x + ORDER[step], 4)
        to_y = lax.rem(here_y + hop, 4)
        return pltpu.make_async_remote_copy(
            src_ref=blocks.at[step, side, pl.ds(pl.multiple_of(to_y * 64, 64), 64)],
            dst_ref=slots.at[step, hop, side],
            send_sem=block_send.at[step, hop, side],
            recv_sem=block_recv.at[step, hop, side],
            device_id={"col": partner if side else col, "row": to_x * 4 + to_y},
            device_id_type=MESH,
        )

    def copies_of(step):
        away = [(hop, side) for hop in (2, 1, 3, 0) for side in (0, 1)]
        return away if step < 3 else away[:6] + [(0, 1)]

    def transform(step):
        to_x = lax.rem(here_x + ORDER[step], 4)
        place = pl.ds(pl.multiple_of(to_x * 256, 256), 256)
        lhs = table[place, :]
        sum_re = jnp.zeros((256, 128), jnp.float32)
        sum_im = jnp.zeros((256, 128), jnp.float32)
        for sub in range(OWN):
            rhs = jnp.concatenate([weights[sub, 0], weights[sub, 1]], axis=1)
            product = jnp.dot(lhs, rhs, preferred_element_type=jnp.float32)
            real, imag = product[:, 0:128], product[:, 128:256]
            row_re, row_im = phase_u[0, sub : sub + 1], phase_u[1, sub : sub + 1]
            mid_re = real * row_re - imag * row_im
            mid_im = real * row_im + imag * row_re
            turn_re, turn_im = phase_v[sub, 0, place], phase_v[sub, 1, place]
            sum_re = sum_re + (mid_re * turn_re - mid_im * turn_im)
            sum_im = sum_im + (mid_re * turn_im + mid_im * turn_re)
        first = jnp.where(low_lanes, sum_re, pltpu.roll(sum_im, 64, 1))
        second = jnp.where(low_lanes, pltpu.roll(sum_re, 64, 1), sum_im)
        mine = jnp.where(core == 0, first, second)
        if step == 3:
            kept[...] = mine
        blocks[step, 0] = mine.astype(jnp.bfloat16)
        blocks[step, 1] = jnp.where(core == 0, second, first).astype(jnp.bfloat16)

    for step in range(4):
        transform(step)
        if step == 0:
            pl.semaphore_wait(barrier, 31)
        for hop, side in copies_of(step):
            block_copy(step, hop, side).start()

    total = kept[pl.ds(pl.multiple_of(here_y * 64, 64), 64), :]
    for step in range(4):
        for hop, side in copies_of(step):
            block_copy(step, hop, side).wait_recv()
            total = total + slots[step, hop, side].astype(jnp.float32)
    result[...] = total
    for step in range(4):
        for hop, side in copies_of(step):
            block_copy(step, hop, side).wait_send()


def per_device(visibility, baseline, offsets, counts, taper_x, taper_y):
    hbm = pl.BlockSpec(memory_space=pltpu.HBM)
    half = jnp.bfloat16
    full = jnp.float32
    total = pl.pallas_call(
        kernel,
        out_shape=jax.ShapeDtypeStruct((64, 128), full),
        in_specs=[hbm] * 7,
        out_specs=pl.BlockSpec(memory_space=pltpu.VMEM),
        scratch_shapes=[
            pltpu.VMEM((OWN, 2, SIDE), full),
            pltpu.VMEM((OWN, 2, SIDE), full),
            pltpu.SMEM((2, 8), jnp.int32),
            pltpu.SMEM((8,), jnp.int32),
            pltpu.VMEM((2, 1, SIDE), full),
            pltpu.VMEM((SIDE, SIDE), half),
            pltpu.VMEM((2 * ROWS, SIDE), half),
            pltpu.VMEM((64, 128), full),
            pltpu.VMEM((24, SIDE), full),
            pltpu.VMEM((8, SIDE, 128), half),
            pltpu.VMEM((8, SIDE, 128), half),
            pltpu.VMEM((2, SIDE, 128), half),
            pltpu.VMEM((OWN, 2, SIDE, 128), half),
            pltpu.VMEM((SIDE, 128), full),
            pltpu.VMEM((2, 8, 128), full),
            pltpu.VMEM((OWN, 2, SIDE, 128), full),
            pltpu.VMEM((256, 128), full),
            pltpu.VMEM((4, 2, 256, 128), half),
            pltpu.VMEM((4, 4, 2, 64, 128), half),
            pltpu.SemaphoreType.DMA((7,)),
            pltpu.SemaphoreType.DMA((4, 4, 2)),
            pltpu.SemaphoreType.DMA((4, 4, 2)),
        ],
        compiler_params=pltpu.CompilerParams(
            collective_id=0, has_side_effects=True, vmem_limit_bytes=48 * 1024 * 1024
        ),
        name="facet_rows",
    )(
        *(
            pltpu.with_memory_space_constraint(array, pltpu.HBM)
            for array in (
                visibility,
                baseline,
                offsets.T,
                counts,
                taper_x.reshape(1, SIDE),
                taper_y.reshape(1, SIDE),
                jnp.asarray(half_table()),
            )
        )
    )
    return total.T.reshape(2, 64, 64)


def solution(mesh):
    placed = (P("row", None, None), P("row", None, None), P("row", None), P("row"), P(), P())
    return jax.shard_map(
        per_device, mesh=mesh, in_specs=placed, out_specs=P(None, "col", "row"), check_vma=False
    )
```

```python
import functools
import math

import jax
import jax.numpy as jnp
import numpy as np
from jax import lax
from jax.experimental import pallas as pl
from jax.experimental.pallas import tpu as pltpu
from jax.sharding import PartitionSpec as P

IMAGE = 32768
SIDE = 1024
HALF = SIDE // 2
STRIDE = IMAGE // SIDE - 1
OWN = 4
ORDER = (2, 3, 1, 0)
ROWS = 128
MESH = pl.DeviceIdType.MESH

COS_POLY = (
    0.9999999890588229,
    -19.73920449945383,
    64.93911745989081,
    -85.45013953079767,
    60.167630950263465,
    -25.967599245923743,
    6.52865815775625,
)


def cos_turns(turns):
    frac = turns - jnp.round(turns)
    square = frac * frac
    value = COS_POLY[6] * square + COS_POLY[5]
    for factor in COS_POLY[4::-1]:
        value = value * square + factor
    return value


def half_table():
    pixel = STRIDE * np.arange(SIDE, dtype=np.int64) - IMAGE // 2
    odd = 2 * np.arange(HALF, dtype=np.int64) + 1
    angle = (2.0 * np.pi / (2 * IMAGE)) * np.mod(pixel[:, None] * odd[None, :], 2 * IMAGE)
    both = np.stack([np.cos(angle).reshape(SIDE, 4, 128), np.sin(angle).reshape(SIDE, 4, 128)], axis=2)
    return both.reshape(SIDE, SIDE).astype(jnp.bfloat16)


def chains(coord, cos_here, sin_here, turns, emit):
    row = lax.broadcasted_iota(jnp.int32, (32, 128), 0).astype(jnp.float32)
    near = row - jnp.broadcast_to(coord, (32, 128))
    multiplier = turns[0:32] * cos_here + turns[32:64] * sin_here

    def anchor(block):
        dist = near + float(32 * block)
        return cos_turns(dist * dist * (1.0 / (2 * SIDE)))

    flip = 7 - lax.broadcasted_iota(jnp.int32, (8, 128), 0)

    def reverse(block):
        pieces = [block[8 * i : 8 * i + 8] for i in range(3, -1, -1)]
        return jnp.concatenate([jnp.take_along_axis(p, flip, axis=0) for p in pieces], axis=0)

    below, above = anchor(15), anchor(16)
    starts = ((multiplier, below, above), tuple(map(reverse, (multiplier, above, below))))
    for part, (factor, before, now) in enumerate(starts):
        for block in range(16):
            emit(part, block, now)
            if block < 15:
                now, before = factor * now - before, now


def kernel(
    visibility_hbm,
    baseline_hbm,
    offsets_hbm,
    counts_hbm,
    taper_x_hbm,
    taper_y_hbm,
    table_hbm,
    result,
    visibility,
    baseline,
    offsets,
    counts,
    taper,
    table,
    own_table,
    turns,
    coords,
    grid_u,
    grid_v,
    weighted,
    weights,
    outgoing,
    incoming,
    advance,
    window,
    sums,
    kept,
    blocks,
    slots,
    load_sem,
    pair_send,
    pair_recv,
    block_send,
    block_recv,
):
    col = lax.axis_index("col")
    row = lax.axis_index("row")
    core = lax.rem(col, 2)
    plane = col // 2
    partner = col + 1 - 2 * core
    here_x = row // 4
    here_y = lax.rem(row, 4)

    own = pl.ds(core * OWN, OWN)
    loads = [
        pltpu.make_async_copy(baseline_hbm.at[own], baseline, load_sem.at[0]),
        pltpu.make_async_copy(offsets_hbm, offsets, load_sem.at[1]),
        pltpu.make_async_copy(taper_x_hbm, taper.at[0], load_sem.at[2]),
        pltpu.make_async_copy(taper_y_hbm, taper.at[1], load_sem.at[3]),
        pltpu.make_async_copy(counts_hbm, counts, load_sem.at[4]),
        pltpu.make_async_copy(visibility_hbm.at[own], visibility, load_sem.at[5]),
        pltpu.make_async_copy(table_hbm, table, load_sem.at[6]),
    ]
    for load in loads:
        load.start()

    barrier = pltpu.get_barrier_semaphore()
    pl.semaphore_signal(barrier, inc=1, device_id={"col": partner, "row": row}, device_id_type=MESH)
    for step in range(1, 16):
        other = lax.rem(row + step, 16)
        pl.semaphore_signal(barrier, inc=1, device_id={"col": col, "row": other}, device_id_type=MESH)

    circle = lax.broadcasted_iota(jnp.int32, (32, 128), 0).astype(jnp.float32) * (1.0 / 32.0)
    turns[0:32] = -2.0 * cos_turns(circle)
    turns[32:64] = -2.0 * cos_turns(circle - 0.25)

    def shift_of(axis, sub):
        which = core * OWN + sub if sub < OWN else (1 - core) * OWN + sub - OWN
        return 2 * offsets[axis, which] + (SIDE - 1)

    def fill_u(sub, block):
        def emit(part, at, value):
            grid_u[block, HALF * part + 32 * at : HALF * part + 32 * at + 32] = value.astype(jnp.bfloat16)

        lanes = pl.ds(block * 128, 128) if isinstance(block, int) else pl.ds(pl.multiple_of(block * 128, 128), 128)
        at = 2 * sub
        chains(coords[at : at + 1, lanes], coords[8 + at : 9 + at, lanes], coords[16 + at : 17 + at, lanes], turns, emit)

    def fill_v(sub, block):
        def emit(part, at, value):
            first = 256 * (at // 4) + 128 * part + 32 * (at % 4)
            grid_v[block, first : first + 32] = value.astype(jnp.bfloat16)

        lanes = pl.ds(block * 128, 128) if isinstance(block, int) else pl.ds(pl.multiple_of(block * 128, 128), 128)
        at = 2 * sub + 1
        chains(coords[at : at + 1, lanes], coords[8 + at : 9 + at, lanes], coords[16 + at : 17 + at, lanes], turns, emit)

    loads[0].wait()
    for sub in range(OWN):
        coords[2 * sub : 2 * sub + 2] = baseline[sub]
    small = coords[0:8] * (1.0 / 32.0)
    coords[8:16] = cos_turns(small)
    coords[16:24] = cos_turns(small - 0.25)

    def first_fill(block, inner):
        fill_u(0, block)
        return inner

    lax.fori_loop(0, 8, first_fill, 0)

    for load in loads[1:]:
        load.wait()

    which_row = lax.broadcasted_iota(jnp.int32, (8, 128), 0)
    shift = jnp.zeros((8, 128), jnp.int32)
    for sub in range(2 * OWN):
        shift = jnp.where(which_row == sub, shift_of(1, sub), shift)
    angle = (8 * STRIDE * shift) & (2 * IMAGE - 1)
    advance[...] = 2.0 * cos_turns(angle.astype(jnp.float32) * (1.0 / (2 * IMAGE)))

    chips = taper[0][:, 0:128]
    for other in range(1, 8):
        chips = jnp.where(plane == other, taper[0][:, 128 * other : 128 * other + 128], chips)
    chips = jnp.broadcast_to(chips, (8, 128))
    turned = pltpu.roll(chips, 64, 1)
    low = lax.broadcasted_iota(jnp.int32, (8, 128), 1) < 64
    scale = 4.0 / (SIDE * math.sqrt(float(128 * SIDE)))
    along_i = jnp.where(core == 0, jnp.where(low, chips, turned), jnp.where(low, turned, chips)) * scale
    columns = taper[1][:, 0:128]
    for other in range(1, 8):
        columns = jnp.where(row // 2 == other, taper[1][:, 128 * other : 128 * other + 128], columns)
    window[...] = jnp.broadcast_to(columns, (128, 128)).T * along_i[0:1]

    for near in range(2):
        place = pl.ds(pl.multiple_of(plane * ROWS + (core if near == 0 else 1 - core) * 64, 64), 64)
        for tile in range(4):
            cos_rows = table[place, 256 * tile : 256 * tile + 128]
            sin_rows = table[place, 256 * tile + 128 : 256 * tile + 256]
            for half, sin_half in ((0, sin_rows), (HALF, -sin_rows)):
                lanes = slice(half + 128 * tile, half + 128 * tile + 128)
                own_table[128 * near : 128 * near + 64, lanes] = cos_rows
                own_table[128 * near + 64 : 128 * near + 128, lanes] = sin_half

    slot = lax.broadcasted_iota(jnp.int32, (2, SIDE), 1)
    for sub in range(OWN):
        mask = slot < counts[core * OWN + sub]
        visibility[sub] = jnp.where(mask, visibility[sub], 0.0)

    def rows_of_image(sub, step):
        rhs = jnp.concatenate([grid_u[2 * step], grid_u[2 * step + 1]], axis=1)
        product = jnp.dot(own_table[...], rhs, preferred_element_type=jnp.float32)
        lanes = pl.ds(step * 256, 256)
        vis_re = visibility[sub, 0:1, lanes]
        vis_im = visibility[sub, 1:2, lanes]
        for near in range(2):
            real = product[128 * near : 128 * near + 64]
            imag = product[128 * near + 64 : 128 * near + 128]
            out_re = real * vis_re - imag * vis_im
            out_im = real * vis_im + imag * vis_re
            weighted[near, lanes, :] = jnp.concatenate([out_re, out_im], axis=0).astype(jnp.bfloat16).T

    sign = jnp.where(lax.broadcasted_iota(jnp.int32, (128, 128), 1) < 64, -1.0, 1.0)

    def columns_of_grid(sub, step):
        place = pl.ds(step * 256, 256)
        lhs = jnp.concatenate([grid_v[i, place, :] for i in range(8)], axis=1)
        rhs = jnp.concatenate([weighted[0], weighted[1]], axis=1)
        product = jnp.dot(lhs, rhs, preferred_element_type=jnp.float32)
        plus, minus = product[0:128], product[128:256]
        for near, target in ((0, weights), (1, outgoing)):
            lanes = slice(128 * near, 128 * near + 128)
            diff = pltpu.roll(plus[:, lanes] - minus[:, lanes], 64, 1) * sign
            target[sub, 256 * step : 256 * step + 128] = (plus[:, lanes] + minus[:, lanes]).astype(jnp.bfloat16)
            target[sub, 256 * step + 128 : 256 * step + 256] = diff.astype(jnp.bfloat16)

    def pair_copy(number):
        some = (pl.ds(0, 2), pl.ds(2, 1), pl.ds(3, 1))[number]
        return pltpu.make_async_remote_copy(
            src_ref=outgoing.at[some],
            dst_ref=incoming.at[some],
            send_sem=pair_send.at[number],
            recv_sem=pair_recv.at[number],
            device_id={"col": partner, "row": row},
            device_id_type=MESH,
        )

    for sub in range(OWN):
        for step in range(4):
            rows_of_image(sub, step)
            fill_v(sub, 2 * step)
            fill_v(sub, 2 * step + 1)
            if sub > 1 and step == 1:
                if sub == 2:
                    pl.semaphore_wait(barrier, 16)
                pair_copy(sub - 2).start()
        for step in range(4):
            columns_of_grid(sub, step)
            if sub + 1 < OWN:
                fill_u(sub + 1, 2 * step)
                fill_u(sub + 1, 2 * step + 1)
    pair_copy(2).start()


    def block_copy(step, hop):
        to_x = lax.rem(here_x + ORDER[step], 4)
        to_y = lax.rem(here_y + hop, 4)
        return pltpu.make_async_remote_copy(
            src_ref=blocks.at[step, pl.ds(pl.multiple_of(to_y * 64, 64), 64)],
            dst_ref=slots.at[step, hop],
            send_sem=block_send.at[step, hop],
            recv_sem=block_recv.at[step, hop],
            device_id={"col": col, "row": to_x * 4 + to_y},
            device_id_type=MESH,
        )

    def hops_of(step):
        return (2, 1, 3, 0) if step < 3 else (2, 1, 3)

    lane = lax.broadcasted_iota(jnp.int32, (8, 128), 1)
    sample = STRIDE * (plane * ROWS + core * 64 + (lane & 63)) - IMAGE // 2
    cross_sign = jnp.where(lane < 64, 1.0, -1.0)

    def transform(step, subs):
        to_x = lax.rem(here_x + ORDER[step], 4)
        place = pl.ds(pl.multiple_of(to_x * 256, 256), 256)
        lhs = table[place, :]
        straight, crossed = [None] * 32, [None] * 32
        if subs[0] > 0:
            straight = [sums[step, 0, 8 * i : 8 * i + 8] for i in range(32)]
            crossed = [sums[step, 1, 8 * i : 8 * i + 8] for i in range(32)]
        for sub in subs:
            rhs = jnp.concatenate([weights[sub], incoming[sub]], axis=1)
            product = jnp.dot(lhs, rhs, preferred_element_type=jnp.float32)
            for side in range(2):
                which = OWN * side + sub
                shift_u, shift_v = shift_of(0, which), shift_of(1, which)
                double = advance[which : which + 1]

                def anchor(at):
                    pixel = STRIDE * (to_x * 256 + 8 * at + which_row) - IMAGE // 2
                    turns = (pixel * shift_v + sample * shift_u) & (2 * IMAGE - 1)
                    frac = turns.astype(jnp.float32) * (1.0 / (2 * IMAGE))
                    return cos_turns(frac), cos_turns(frac - 0.25) * cross_sign

                below, above = anchor(15), anchor(16)
                for before, now, order in ((below, above, range(16, 32)), (above, below, range(15, -1, -1))):
                    for at in order:
                        part = product[8 * at : 8 * at + 8, 128 * side : 128 * side + 128]
                        add, cross = part * now[0], part * now[1]
                        straight[at] = add if straight[at] is None else straight[at] + add
                        crossed[at] = cross if crossed[at] is None else crossed[at] + cross
                        after = tuple(double * b - a for a, b in zip(before, now))
                        before, now = now, after
        if subs[-1] < OWN - 1:
            sums[step, 0] = jnp.concatenate(straight, axis=0)
            sums[step, 1] = jnp.concatenate(crossed, axis=0)
            return
        total = jnp.concatenate(straight, axis=0) + pltpu.roll(jnp.concatenate(crossed, axis=0), 64, 1)
        if step == 3:
            kept[...] = total
        blocks[step] = total.astype(jnp.bfloat16)

    early, late = (0, 1, 2), (3,)
    pair_copy(0).wait_recv()
    pair_copy(1).wait_recv()
    for step in range(4):
        transform(step, early)
    pair_copy(2).wait_recv()
    for steps in ((0, 1), (2, 3)):
        for step in steps:
            transform(step, late)
        for step in steps:
            for hop in hops_of(step):
                block_copy(step, hop).start()

    total = kept[pl.ds(pl.multiple_of(here_y * 64, 64), 64), :]
    for step in range(4):
        for hop in hops_of(step):
            block_copy(step, hop).wait_recv()
            total = total + slots[step, hop].astype(jnp.float32)
    result[...] = total * window[pl.ds(pl.multiple_of(lax.rem(row, 2) * 64, 64), 64), :]
    for number in range(3):
        pair_copy(number).wait_send()
    for step in range(4):
        for hop in hops_of(step):
            block_copy(step, hop).wait_send()


def per_device(visibility, baseline, offsets, counts, taper_x, taper_y):
    hbm = pl.BlockSpec(memory_space=pltpu.HBM)
    half = jnp.bfloat16
    full = jnp.float32
    total = pl.pallas_call(
        kernel,
        out_shape=jax.ShapeDtypeStruct((64, 128), full),
        in_specs=[hbm] * 7,
        out_specs=pl.BlockSpec(memory_space=pltpu.VMEM),
        scratch_shapes=[
            pltpu.VMEM((OWN, 2, SIDE), full),
            pltpu.VMEM((OWN, 2, SIDE), full),
            pltpu.SMEM((2, 8), jnp.int32),
            pltpu.SMEM((8,), jnp.int32),
            pltpu.VMEM((2, 1, SIDE), full),
            pltpu.VMEM((SIDE, SIDE), half),
            pltpu.VMEM((2 * ROWS, SIDE), half),
            pltpu.VMEM((64, 128), full),
            pltpu.VMEM((24, SIDE), full),
            pltpu.VMEM((8, SIDE, 128), half),
            pltpu.VMEM((8, SIDE, 128), half),
            pltpu.VMEM((2, SIDE, 128), half),
            pltpu.VMEM((OWN, SIDE, 128), half),
            pltpu.VMEM((OWN, SIDE, 128), half),
            pltpu.VMEM((OWN, SIDE, 128), half),
            pltpu.VMEM((8, 128), full),
            pltpu.VMEM((128, 128), full),
            pltpu.VMEM((4, 2, 256, 128), full),
            pltpu.VMEM((256, 128), full),
            pltpu.VMEM((4, 256, 128), half),
            pltpu.VMEM((4, 4, 64, 128), half),
            pltpu.SemaphoreType.DMA((7,)),
            pltpu.SemaphoreType.DMA((3,)),
            pltpu.SemaphoreType.DMA((3,)),
            pltpu.SemaphoreType.DMA((4, 4)),
            pltpu.SemaphoreType.DMA((4, 4)),
        ],
        compiler_params=pltpu.CompilerParams(
            collective_id=0, has_side_effects=True, vmem_limit_bytes=48 * 1024 * 1024
        ),
        name="facet_rows",
    )(
        *(
            pltpu.with_memory_space_constraint(array, pltpu.HBM)
            for array in (
                visibility,
                baseline,
                offsets.T,
                counts,
                taper_x.reshape(1, SIDE),
                taper_y.reshape(1, SIDE),
                jnp.asarray(half_table()),
            )
        )
    )
    return total.T.reshape(2, 64, 64)


def solution(mesh):
    placed = (P("row", None, None), P("row", None, None), P("row", None), P("row"), P(), P())
    return jax.shard_map(
        per_device, mesh=mesh, in_specs=placed, out_specs=P(None, "col", "row"), check_vma=False
    )
```

```python
import functools
import math

import jax
import jax.numpy as jnp
import numpy as np
from jax import lax
from jax.experimental import pallas as pl
from jax.experimental.pallas import tpu as pltpu
from jax.sharding import PartitionSpec as P

IMAGE = 32768
SIDE = 1024
HALF = SIDE // 2
STRIDE = IMAGE // SIDE - 1
OWN = 4
ORDER = (2, 3, 1, 0)
ROWS = 128
MESH = pl.DeviceIdType.MESH

COS_POLY = (
    0.9999999890588229,
    -19.73920449945383,
    64.93911745989081,
    -85.45013953079767,
    60.167630950263465,
    -25.967599245923743,
    6.52865815775625,
)


def cos_turns(turns):
    frac = turns - jnp.round(turns)
    square = frac * frac
    value = COS_POLY[6] * square + COS_POLY[5]
    for factor in COS_POLY[4::-1]:
        value = value * square + factor
    return value


def half_table():
    pixel = STRIDE * np.arange(SIDE, dtype=np.int64) - IMAGE // 2
    odd = 2 * np.arange(HALF, dtype=np.int64) + 1
    angle = (2.0 * np.pi / (2 * IMAGE)) * np.mod(pixel[:, None] * odd[None, :], 2 * IMAGE)
    both = np.stack([np.cos(angle).reshape(SIDE, 4, 128), np.sin(angle).reshape(SIDE, 4, 128)], axis=2)
    return both.reshape(SIDE, SIDE).astype(jnp.bfloat16)


def chains(rows, turns, emit):
    coord, cos_32, sin_32, cos_128, sin_128 = rows
    multiplier = turns[0:32] * cos_32 + turns[32:64] * sin_32
    crossing = turns[32:64] * cos_32 - turns[0:32] * sin_32

    dist = (lax.broadcasted_iota(jnp.int32, (8, 128), 0).astype(jnp.float32) + 480.0) - coord
    turn = dist * dist * (1.0 / (2 * SIDE))
    cos_now, sin_now = cos_turns(turn), cos_turns(turn - 0.25)
    cosines, sines = [cos_now], [sin_now]
    for step in range(3):
        cos_at, sin_at = turns[64 + 16 * step : 72 + 16 * step], turns[72 + 16 * step : 80 + 16 * step]
        cos_step = cos_at * cos_128 + sin_at * sin_128
        sin_step = sin_at * cos_128 - cos_at * sin_128
        cos_now, sin_now = cos_now * cos_step - sin_now * sin_step, sin_now * cos_step + cos_now * sin_step
        cosines.append(cos_now)
        sines.append(sin_now)
    below = jnp.concatenate(cosines, axis=0)
    above = 0.5 * (below * multiplier - jnp.concatenate(sines, axis=0) * crossing)

    flip = 7 - lax.broadcasted_iota(jnp.int32, (8, 128), 0)

    def reverse(block):
        pieces = [block[8 * i : 8 * i + 8] for i in range(3, -1, -1)]
        return jnp.concatenate([jnp.take_along_axis(p, flip, axis=0) for p in pieces], axis=0)

    starts = ((multiplier, below, above), tuple(map(reverse, (multiplier, above, below))))
    for part, (factor, before, now) in enumerate(starts):
        for block in range(16):
            emit(part, block, now)
            if block < 15:
                now, before = factor * now - before, now


def kernel(
    visibility_hbm,
    baseline_hbm,
    offsets_hbm,
    counts_hbm,
    taper_x_hbm,
    taper_y_hbm,
    table_hbm,
    result,
    visibility,
    baseline,
    offsets,
    counts,
    taper,
    table,
    own_table,
    turns,
    coords,
    grid_u,
    grid_v,
    weighted,
    weights,
    outgoing,
    incoming,
    advance,
    window,
    sums,
    kept,
    blocks,
    slots,
    load_sem,
    pair_send,
    pair_recv,
    block_send,
    block_recv,
):
    col = lax.axis_index("col")
    row = lax.axis_index("row")
    core = lax.rem(col, 2)
    plane = col // 2
    partner = col + 1 - 2 * core
    here_x = row // 4
    here_y = lax.rem(row, 4)

    own = pl.ds(core * OWN, OWN)
    loads = [
        pltpu.make_async_copy(baseline_hbm.at[own], baseline, load_sem.at[0]),
        pltpu.make_async_copy(offsets_hbm, offsets, load_sem.at[1]),
        pltpu.make_async_copy(taper_x_hbm, taper.at[0], load_sem.at[2]),
        pltpu.make_async_copy(taper_y_hbm, taper.at[1], load_sem.at[3]),
        pltpu.make_async_copy(counts_hbm, counts, load_sem.at[4]),
        pltpu.make_async_copy(visibility_hbm.at[own], visibility, load_sem.at[5]),
        pltpu.make_async_copy(table_hbm, table, load_sem.at[6]),
    ]
    for load in loads:
        load.start()

    barrier = pltpu.get_barrier_semaphore()
    pl.semaphore_signal(barrier, inc=1, device_id={"col": partner, "row": row}, device_id_type=MESH)
    for step in range(1, 16):
        other = lax.rem(row + step, 16)
        pl.semaphore_signal(barrier, inc=1, device_id={"col": col, "row": other}, device_id_type=MESH)

    circle = lax.broadcasted_iota(jnp.int32, (32, 128), 0).astype(jnp.float32) * (1.0 / 32.0)
    turns[0:32] = -2.0 * cos_turns(circle)
    turns[32:64] = -2.0 * cos_turns(circle - 0.25)
    eighth = (lax.broadcasted_iota(jnp.int32, (8, 128), 0).astype(jnp.float32) + 484.0) * (1.0 / 128.0)
    for step in range(3):
        turns[64 + 16 * step : 72 + 16 * step] = cos_turns(eighth + step / 16.0)
        turns[72 + 16 * step : 80 + 16 * step] = cos_turns(eighth + (step / 16.0 - 0.25))

    def shift_of(axis, sub):
        which = core * OWN + sub if sub < OWN else (1 - core) * OWN + sub - OWN
        return 2 * offsets[axis, which] + (SIDE - 1)

    def fill_u(sub, block):
        def emit(part, at, value):
            grid_u[block, HALF * part + 32 * at : HALF * part + 32 * at + 32] = value.astype(jnp.bfloat16)

        lanes = pl.ds(block * 128, 128) if isinstance(block, int) else pl.ds(pl.multiple_of(block * 128, 128), 128)
        at = 2 * sub
        chains([coords[8 * i + at : 8 * i + at + 1, lanes] for i in range(5)], turns, emit)

    def fill_v(sub, block):
        def emit(part, at, value):
            first = 256 * (at // 4) + 128 * part + 32 * (at % 4)
            grid_v[block, first : first + 32] = value.astype(jnp.bfloat16)

        lanes = pl.ds(block * 128, 128) if isinstance(block, int) else pl.ds(pl.multiple_of(block * 128, 128), 128)
        at = 2 * sub + 1
        chains([coords[8 * i + at : 8 * i + at + 1, lanes] for i in range(5)], turns, emit)

    loads[0].wait()
    for sub in range(OWN):
        coords[2 * sub : 2 * sub + 2] = baseline[sub]
    small = coords[0:8] * (1.0 / 32.0)
    coords[8:16] = cos_turns(small)
    coords[16:24] = cos_turns(small - 0.25)
    small = coords[0:8] * (1.0 / 128.0)
    coords[24:32] = cos_turns(small)
    coords[32:40] = cos_turns(small - 0.25)

    def first_fill(block, inner):
        fill_u(0, block)
        return inner

    lax.fori_loop(0, 8, first_fill, 0)

    for load in loads[1:]:
        load.wait()

    which_row = lax.broadcasted_iota(jnp.int32, (8, 128), 0)
    shift = jnp.zeros((8, 128), jnp.int32)
    for sub in range(2 * OWN):
        shift = jnp.where(which_row == sub, shift_of(1, sub), shift)
    angle = (8 * STRIDE * shift) & (2 * IMAGE - 1)
    advance[...] = 2.0 * cos_turns(angle.astype(jnp.float32) * (1.0 / (2 * IMAGE)))

    chips = taper[0][:, 0:128]
    for other in range(1, 8):
        chips = jnp.where(plane == other, taper[0][:, 128 * other : 128 * other + 128], chips)
    chips = jnp.broadcast_to(chips, (8, 128))
    turned = pltpu.roll(chips, 64, 1)
    low = lax.broadcasted_iota(jnp.int32, (8, 128), 1) < 64
    scale = 4.0 / (SIDE * math.sqrt(float(128 * SIDE)))
    along_i = jnp.where(core == 0, jnp.where(low, chips, turned), jnp.where(low, turned, chips)) * scale
    columns = taper[1][:, 0:128]
    for other in range(1, 8):
        columns = jnp.where(row // 2 == other, taper[1][:, 128 * other : 128 * other + 128], columns)
    window[...] = jnp.broadcast_to(columns, (128, 128)).T * along_i[0:1]

    for near in range(2):
        place = pl.ds(pl.multiple_of(plane * ROWS + (core if near == 0 else 1 - core) * 64, 64), 64)
        for tile in range(4):
            cos_rows = table[place, 256 * tile : 256 * tile + 128]
            sin_rows = table[place, 256 * tile + 128 : 256 * tile + 256]
            for half, sin_half in ((0, sin_rows), (HALF, -sin_rows)):
                lanes = slice(half + 128 * tile, half + 128 * tile + 128)
                own_table[128 * near : 128 * near + 64, lanes] = cos_rows
                own_table[128 * near + 64 : 128 * near + 128, lanes] = sin_half

    slot = lax.broadcasted_iota(jnp.int32, (2, SIDE), 1)
    for sub in range(OWN):
        mask = slot < counts[core * OWN + sub]
        visibility[sub] = jnp.where(mask, visibility[sub], 0.0)

    def rows_of_image(sub, step):
        rhs = jnp.concatenate([grid_u[2 * step], grid_u[2 * step + 1]], axis=1)
        product = jnp.dot(own_table[...], rhs, preferred_element_type=jnp.float32)
        lanes = pl.ds(step * 256, 256)
        vis_re = visibility[sub, 0:1, lanes]
        vis_im = visibility[sub, 1:2, lanes]
        for near in range(2):
            real = product[128 * near : 128 * near + 64]
            imag = product[128 * near + 64 : 128 * near + 128]
            out_re = real * vis_re - imag * vis_im
            out_im = real * vis_im + imag * vis_re
            weighted[near, lanes, :] = jnp.concatenate([out_re, out_im], axis=0).astype(jnp.bfloat16).T

    sign = jnp.where(lax.broadcasted_iota(jnp.int32, (128, 128), 1) < 64, -1.0, 1.0)

    def columns_of_grid(sub, step):
        place = pl.ds(step * 256, 256)
        lhs = jnp.concatenate([grid_v[i, place, :] for i in range(8)], axis=1)
        rhs = jnp.concatenate([weighted[0], weighted[1]], axis=1)
        product = jnp.dot(lhs, rhs, preferred_element_type=jnp.float32)
        plus, minus = product[0:128], product[128:256]
        for near, target in ((0, weights), (1, outgoing)):
            lanes = slice(128 * near, 128 * near + 128)
            diff = pltpu.roll(plus[:, lanes] - minus[:, lanes], 64, 1) * sign
            target[sub, 256 * step : 256 * step + 128] = (plus[:, lanes] + minus[:, lanes]).astype(jnp.bfloat16)
            target[sub, 256 * step + 128 : 256 * step + 256] = diff.astype(jnp.bfloat16)

    def pair_copy(number):
        some = (pl.ds(0, 2), pl.ds(2, 1), pl.ds(3, 1))[number]
        return pltpu.make_async_remote_copy(
            src_ref=outgoing.at[some],
            dst_ref=incoming.at[some],
            send_sem=pair_send.at[number],
            recv_sem=pair_recv.at[number],
            device_id={"col": partner, "row": row},
            device_id_type=MESH,
        )

    for sub in range(OWN):
        for step in range(4):
            rows_of_image(sub, step)
            fill_v(sub, 2 * step)
            fill_v(sub, 2 * step + 1)
            if sub > 1 and step == 1:
                if sub == 2:
                    pl.semaphore_wait(barrier, 16)
                pair_copy(sub - 2).start()
        for step in range(4):
            columns_of_grid(sub, step)
            if sub + 1 < OWN:
                fill_u(sub + 1, 2 * step)
                fill_u(sub + 1, 2 * step + 1)
    pair_copy(2).start()


    def block_copy(step, hop):
        to_x = lax.rem(here_x + ORDER[step], 4)
        to_y = lax.rem(here_y + hop, 4)
        return pltpu.make_async_remote_copy(
            src_ref=blocks.at[step, pl.ds(pl.multiple_of(to_y * 64, 64), 64)],
            dst_ref=slots.at[step, hop],
            send_sem=block_send.at[step, hop],
            recv_sem=block_recv.at[step, hop],
            device_id={"col": col, "row": to_x * 4 + to_y},
            device_id_type=MESH,
        )

    def hops_of(step):
        return (2, 1, 3, 0) if step < 3 else (2, 1, 3)

    lane = lax.broadcasted_iota(jnp.int32, (8, 128), 1)
    sample = STRIDE * (plane * ROWS + core * 64 + (lane & 63)) - IMAGE // 2
    cross_sign = jnp.where(lane < 64, 1.0, -1.0)

    def transform(step, subs):
        to_x = lax.rem(here_x + ORDER[step], 4)
        place = pl.ds(pl.multiple_of(to_x * 256, 256), 256)
        lhs = table[place, :]
        straight, crossed = [None] * 32, [None] * 32
        if subs[0] > 0:
            straight = [sums[step, 0, 8 * i : 8 * i + 8] for i in range(32)]
            crossed = [sums[step, 1, 8 * i : 8 * i + 8] for i in range(32)]
        for sub in subs:
            rhs = jnp.concatenate([weights[sub], incoming[sub]], axis=1)
            product = jnp.dot(lhs, rhs, preferred_element_type=jnp.float32)
            for side in range(2):
                which = OWN * side + sub
                shift_u, shift_v = shift_of(0, which), shift_of(1, which)
                double = advance[which : which + 1]

                def anchor(at):
                    pixel = STRIDE * (to_x * 256 + 8 * at + which_row) - IMAGE // 2
                    turns = (pixel * shift_v + sample * shift_u) & (2 * IMAGE - 1)
                    frac = turns.astype(jnp.float32) * (1.0 / (2 * IMAGE))
                    return cos_turns(frac), cos_turns(frac - 0.25) * cross_sign

                below, above = anchor(15), anchor(16)
                for before, now, order in ((below, above, range(16, 32)), (above, below, range(15, -1, -1))):
                    for at in order:
                        part = product[8 * at : 8 * at + 8, 128 * side : 128 * side + 128]
                        add, cross = part * now[0], part * now[1]
                        straight[at] = add if straight[at] is None else straight[at] + add
                        crossed[at] = cross if crossed[at] is None else crossed[at] + cross
                        after = tuple(double * b - a for a, b in zip(before, now))
                        before, now = now, after
        if subs[-1] < OWN - 1:
            sums[step, 0] = jnp.concatenate(straight, axis=0)
            sums[step, 1] = jnp.concatenate(crossed, axis=0)
            return
        total = jnp.concatenate(straight, axis=0) + pltpu.roll(jnp.concatenate(crossed, axis=0), 64, 1)
        if step == 3:
            kept[...] = total
        blocks[step] = total.astype(jnp.bfloat16)

    early, late = (0, 1, 2), (3,)
    pair_copy(0).wait_recv()
    pair_copy(1).wait_recv()
    for step in range(4):
        transform(step, early)
    pair_copy(2).wait_recv()
    for steps in ((0, 1), (2, 3)):
        for step in steps:
            transform(step, late)
        for step in steps:
            for hop in hops_of(step):
                block_copy(step, hop).start()

    total = kept[pl.ds(pl.multiple_of(here_y * 64, 64), 64), :]
    for step in range(4):
        for hop in hops_of(step):
            block_copy(step, hop).wait_recv()
    for step in range(4):
        for hop in hops_of(step):
            total = total + slots[step, hop].astype(jnp.float32)
    result[...] = total * window[pl.ds(pl.multiple_of(lax.rem(row, 2) * 64, 64), 64), :]
    for number in range(3):
        pair_copy(number).wait_send()
    for step in range(4):
        for hop in hops_of(step):
            block_copy(step, hop).wait_send()


def per_device(visibility, baseline, offsets, counts, taper_x, taper_y):
    hbm = pl.BlockSpec(memory_space=pltpu.HBM)
    half = jnp.bfloat16
    full = jnp.float32
    total = pl.pallas_call(
        kernel,
        out_shape=jax.ShapeDtypeStruct((64, 128), full),
        in_specs=[hbm] * 7,
        out_specs=pl.BlockSpec(memory_space=pltpu.VMEM),
        scratch_shapes=[
            pltpu.VMEM((OWN, 2, SIDE), full),
            pltpu.VMEM((OWN, 2, SIDE), full),
            pltpu.SMEM((2, 8), jnp.int32),
            pltpu.SMEM((8,), jnp.int32),
            pltpu.VMEM((2, 1, SIDE), full),
            pltpu.VMEM((SIDE, SIDE), half),
            pltpu.VMEM((2 * ROWS, SIDE), half),
            pltpu.VMEM((112, 128), full),
            pltpu.VMEM((40, SIDE), full),
            pltpu.VMEM((8, SIDE, 128), half),
            pltpu.VMEM((8, SIDE, 128), half),
            pltpu.VMEM((2, SIDE, 128), half),
            pltpu.VMEM((OWN, SIDE, 128), half),
            pltpu.VMEM((OWN, SIDE, 128), half),
            pltpu.VMEM((OWN, SIDE, 128), half),
            pltpu.VMEM((8, 128), full),
            pltpu.VMEM((128, 128), full),
            pltpu.VMEM((4, 2, 256, 128), full),
            pltpu.VMEM((256, 128), full),
            pltpu.VMEM((4, 256, 128), half),
            pltpu.VMEM((4, 4, 64, 128), half),
            pltpu.SemaphoreType.DMA((7,)),
            pltpu.SemaphoreType.DMA((3,)),
            pltpu.SemaphoreType.DMA((3,)),
            pltpu.SemaphoreType.DMA((4, 4)),
            pltpu.SemaphoreType.DMA((4, 4)),
        ],
        compiler_params=pltpu.CompilerParams(
            collective_id=0, has_side_effects=True, vmem_limit_bytes=48 * 1024 * 1024
        ),
        name="facet_rows",
    )(
        *(
            pltpu.with_memory_space_constraint(array, pltpu.HBM)
            for array in (
                visibility,
                baseline,
                offsets.T,
                counts,
                taper_x.reshape(1, SIDE),
                taper_y.reshape(1, SIDE),
                jnp.asarray(half_table()),
            )
        )
    )
    return total.T.reshape(2, 64, 64)


def solution(mesh):
    placed = (P("row", None, None), P("row", None, None), P("row", None), P("row"), P(), P())
    return jax.shard_map(
        per_device, mesh=mesh, in_specs=placed, out_specs=P(None, "col", "row"), check_vma=False
    )
```

```python
import functools
import math

import jax
import jax.numpy as jnp
import numpy as np
from jax import lax
from jax.experimental import pallas as pl
from jax.experimental.pallas import tpu as pltpu
from jax.sharding import PartitionSpec as P

IMAGE = 32768
SIDE = 1024
HALF = SIDE // 2
STRIDE = IMAGE // SIDE - 1
OWN = 4
ORDER = (2, 3, 1, 0)
ROWS = 128
MESH = pl.DeviceIdType.MESH

COS_POLY = (
    0.9999999890588229,
    -19.73920449945383,
    64.93911745989081,
    -85.45013953079767,
    60.167630950263465,
    -25.967599245923743,
    6.52865815775625,
)


def cos_turns(turns):
    frac = turns - jnp.round(turns)
    square = frac * frac
    value = COS_POLY[6] * square + COS_POLY[5]
    for factor in COS_POLY[4::-1]:
        value = value * square + factor
    return value


def half_table():
    pixel = STRIDE * np.arange(SIDE, dtype=np.int64) - IMAGE // 2
    odd = 2 * np.arange(HALF, dtype=np.int64) + 1
    angle = (2.0 * np.pi / (2 * IMAGE)) * np.mod(pixel[:, None] * odd[None, :], 2 * IMAGE)
    both = np.stack([np.cos(angle).reshape(SIDE, 4, 128), np.sin(angle).reshape(SIDE, 4, 128)], axis=2)
    return both.reshape(SIDE, SIDE).astype(jnp.bfloat16)


def chains(rows, turns, emit):
    coord, cos_32, sin_32, cos_128, sin_128 = rows
    multiplier = turns[0:32] * cos_32 + turns[32:64] * sin_32
    crossing = turns[32:64] * cos_32 - turns[0:32] * sin_32

    dist = (lax.broadcasted_iota(jnp.int32, (8, 128), 0).astype(jnp.float32) + 480.0) - coord
    turn = dist * dist * (1.0 / (2 * SIDE))
    cos_now, sin_now = cos_turns(turn), cos_turns(turn - 0.25)
    cosines, sines = [cos_now], [sin_now]
    for step in range(3):
        cos_at, sin_at = turns[64 + 16 * step : 72 + 16 * step], turns[72 + 16 * step : 80 + 16 * step]
        cos_step = cos_at * cos_128 + sin_at * sin_128
        sin_step = sin_at * cos_128 - cos_at * sin_128
        cos_now, sin_now = cos_now * cos_step - sin_now * sin_step, sin_now * cos_step + cos_now * sin_step
        cosines.append(cos_now)
        sines.append(sin_now)
    below = jnp.concatenate(cosines, axis=0)
    above = 0.5 * (below * multiplier - jnp.concatenate(sines, axis=0) * crossing)

    flip = 7 - lax.broadcasted_iota(jnp.int32, (8, 128), 0)

    def reverse(block):
        pieces = [block[8 * i : 8 * i + 8] for i in range(3, -1, -1)]
        return jnp.concatenate([jnp.take_along_axis(p, flip, axis=0) for p in pieces], axis=0)

    starts = ((multiplier, below, above), tuple(map(reverse, (multiplier, above, below))))
    for part, (factor, before, now) in enumerate(starts):
        for block in range(16):
            emit(part, block, now)
            if block < 15:
                now, before = factor * now - before, now


def kernel(
    visibility_hbm,
    baseline_hbm,
    offsets_hbm,
    counts_hbm,
    taper_x_hbm,
    taper_y_hbm,
    table_hbm,
    result,
    visibility,
    baseline,
    offsets,
    counts,
    taper,
    table,
    own_table,
    turns,
    coords,
    grid_u,
    grid_v,
    weighted,
    weights,
    outgoing,
    incoming,
    advance,
    window,
    sums,
    kept,
    blocks,
    slots,
    load_sem,
    pair_send,
    pair_recv,
    block_send,
    block_recv,
):
    col = lax.axis_index("col")
    row = lax.axis_index("row")
    core = lax.rem(col, 2)
    plane = col // 2
    partner = col + 1 - 2 * core
    here_x = row // 4
    here_y = lax.rem(row, 4)

    own = pl.ds(core * OWN, OWN)
    loads = [
        pltpu.make_async_copy(baseline_hbm.at[own], baseline, load_sem.at[0]),
        pltpu.make_async_copy(offsets_hbm, offsets, load_sem.at[1]),
        pltpu.make_async_copy(taper_x_hbm, taper.at[0], load_sem.at[2]),
        pltpu.make_async_copy(taper_y_hbm, taper.at[1], load_sem.at[3]),
        pltpu.make_async_copy(counts_hbm, counts, load_sem.at[4]),
        pltpu.make_async_copy(visibility_hbm.at[own], visibility, load_sem.at[5]),
        pltpu.make_async_copy(table_hbm, table, load_sem.at[6]),
    ]
    for load in loads:
        load.start()

    barrier = pltpu.get_barrier_semaphore()
    pl.semaphore_signal(barrier, inc=1, device_id={"col": partner, "row": row}, device_id_type=MESH)
    for step in range(1, 16):
        other = lax.rem(row + step, 16)
        pl.semaphore_signal(barrier, inc=1, device_id={"col": col, "row": other}, device_id_type=MESH)

    circle = lax.broadcasted_iota(jnp.int32, (32, 128), 0).astype(jnp.float32) * (1.0 / 32.0)
    turns[0:32] = -2.0 * cos_turns(circle)
    turns[32:64] = -2.0 * cos_turns(circle - 0.25)
    eighth = (lax.broadcasted_iota(jnp.int32, (8, 128), 0).astype(jnp.float32) + 484.0) * (1.0 / 128.0)
    for step in range(3):
        turns[64 + 16 * step : 72 + 16 * step] = cos_turns(eighth + step / 16.0)
        turns[72 + 16 * step : 80 + 16 * step] = cos_turns(eighth + (step / 16.0 - 0.25))

    def shift_of(axis, sub):
        which = core * OWN + sub if sub < OWN else (1 - core) * OWN + sub - OWN
        return 2 * offsets[axis, which] + (SIDE - 1)

    def fill_u(sub, block):
        def emit(part, at, value):
            grid_u[block, HALF * part + 32 * at : HALF * part + 32 * at + 32] = value.astype(jnp.bfloat16)

        lanes = pl.ds(block * 128, 128) if isinstance(block, int) else pl.ds(pl.multiple_of(block * 128, 128), 128)
        at = 2 * sub
        chains([coords[8 * i + at : 8 * i + at + 1, lanes] for i in range(5)], turns, emit)

    def fill_v(sub, block):
        def emit(part, at, value):
            first = 256 * (at // 4) + 128 * part + 32 * (at % 4)
            grid_v[block, first : first + 32] = value.astype(jnp.bfloat16)

        lanes = pl.ds(block * 128, 128) if isinstance(block, int) else pl.ds(pl.multiple_of(block * 128, 128), 128)
        at = 2 * sub + 1
        chains([coords[8 * i + at : 8 * i + at + 1, lanes] for i in range(5)], turns, emit)

    loads[0].wait()
    for sub in range(OWN):
        coords[2 * sub : 2 * sub + 2] = baseline[sub]
    small = coords[0:8] * (1.0 / 32.0)
    coords[8:16] = cos_turns(small)
    coords[16:24] = cos_turns(small - 0.25)
    small = coords[0:8] * (1.0 / 128.0)
    coords[24:32] = cos_turns(small)
    coords[32:40] = cos_turns(small - 0.25)

    def first_fill(block, inner):
        fill_u(0, block)
        return inner

    lax.fori_loop(0, 8, first_fill, 0)

    for load in loads[1:]:
        load.wait()

    which_row = lax.broadcasted_iota(jnp.int32, (8, 128), 0)
    shift = jnp.zeros((8, 128), jnp.int32)
    for sub in range(2 * OWN):
        shift = jnp.where(which_row == sub, shift_of(1, sub), shift)
    angle = (8 * STRIDE * shift) & (2 * IMAGE - 1)
    advance[...] = 2.0 * cos_turns(angle.astype(jnp.float32) * (1.0 / (2 * IMAGE)))

    chips = taper[0][:, 0:128]
    for other in range(1, 8):
        chips = jnp.where(plane == other, taper[0][:, 128 * other : 128 * other + 128], chips)
    chips = jnp.broadcast_to(chips, (8, 128))
    turned = pltpu.roll(chips, 64, 1)
    low = lax.broadcasted_iota(jnp.int32, (8, 128), 1) < 64
    scale = 4.0 / (SIDE * math.sqrt(float(128 * SIDE)))
    along_i = jnp.where(core == 0, jnp.where(low, chips, turned), jnp.where(low, turned, chips)) * scale
    columns = taper[1][:, 0:128]
    for other in range(1, 8):
        columns = jnp.where(row // 2 == other, taper[1][:, 128 * other : 128 * other + 128], columns)
    window[...] = jnp.broadcast_to(columns, (128, 128)).T * along_i[0:1]

    for near in range(2):
        place = pl.ds(pl.multiple_of(plane * ROWS + (core if near == 0 else 1 - core) * 64, 64), 64)
        for tile in range(4):
            cos_rows = table[place, 256 * tile : 256 * tile + 128]
            sin_rows = table[place, 256 * tile + 128 : 256 * tile + 256]
            for half, sin_half in ((0, sin_rows), (HALF, -sin_rows)):
                lanes = slice(half + 128 * tile, half + 128 * tile + 128)
                own_table[128 * near : 128 * near + 64, lanes] = cos_rows
                own_table[128 * near + 64 : 128 * near + 128, lanes] = sin_half

    slot = lax.broadcasted_iota(jnp.int32, (2, SIDE), 1)
    for sub in range(OWN):
        mask = slot < counts[core * OWN + sub]
        visibility[sub] = jnp.where(mask, visibility[sub], 0.0)

    def rows_of_image(sub, step):
        rhs = jnp.concatenate([grid_u[2 * step], grid_u[2 * step + 1]], axis=1)
        product = jnp.dot(own_table[...], rhs, preferred_element_type=jnp.float32)
        lanes = pl.ds(step * 256, 256)
        vis_re = visibility[sub, 0:1, lanes]
        vis_im = visibility[sub, 1:2, lanes]
        for near in range(2):
            real = product[128 * near : 128 * near + 64]
            imag = product[128 * near + 64 : 128 * near + 128]
            out_re = real * vis_re - imag * vis_im
            out_im = real * vis_im + imag * vis_re
            weighted[near, lanes, :] = jnp.concatenate([out_re, out_im], axis=0).astype(jnp.bfloat16).T

    sign = jnp.where(lax.broadcasted_iota(jnp.int32, (128, 128), 1) < 64, -1.0, 1.0)

    def columns_of_grid(sub, step):
        place = pl.ds(step * 256, 256)
        lhs = jnp.concatenate([grid_v[i, place, :] for i in range(8)], axis=1)
        rhs = jnp.concatenate([weighted[0], weighted[1]], axis=1)
        product = jnp.dot(lhs, rhs, preferred_element_type=jnp.float32)
        plus, minus = product[0:128], product[128:256]
        for near, target in ((0, weights), (1, outgoing)):
            lanes = slice(128 * near, 128 * near + 128)
            diff = pltpu.roll(plus[:, lanes] - minus[:, lanes], 64, 1) * sign
            target[sub, 256 * step : 256 * step + 128] = (plus[:, lanes] + minus[:, lanes]).astype(jnp.bfloat16)
            target[sub, 256 * step + 128 : 256 * step + 256] = diff.astype(jnp.bfloat16)

    def pair_copy(number):
        some = (pl.ds(0, 2), pl.ds(2, 1), pl.ds(3, 1))[number]
        return pltpu.make_async_remote_copy(
            src_ref=outgoing.at[some],
            dst_ref=incoming.at[some],
            send_sem=pair_send.at[number],
            recv_sem=pair_recv.at[number],
            device_id={"col": partner, "row": row},
            device_id_type=MESH,
        )

    for sub in range(OWN):
        for step in range(4):
            rows_of_image(sub, step)
            fill_v(sub, 2 * step)
            fill_v(sub, 2 * step + 1)
            if sub > 1 and step == 1:
                if sub == 2:
                    pl.semaphore_wait(barrier, 16)
                pair_copy(sub - 2).start()
        for step in range(4):
            columns_of_grid(sub, step)
            if sub + 1 < OWN:
                fill_u(sub + 1, 2 * step)
                fill_u(sub + 1, 2 * step + 1)
    pair_copy(2).start()


    def block_copy(step, hop):
        to_x = lax.rem(here_x + ORDER[step], 4)
        to_y = lax.rem(here_y + hop, 4)
        return pltpu.make_async_remote_copy(
            src_ref=blocks.at[step, pl.ds(pl.multiple_of(to_y * 64, 64), 64)],
            dst_ref=slots.at[step, hop],
            send_sem=block_send.at[step, hop],
            recv_sem=block_recv.at[step, hop],
            device_id={"col": col, "row": to_x * 4 + to_y},
            device_id_type=MESH,
        )

    def hops_of(step):
        return (2, 1, 3, 0) if step < 3 else (2, 1, 3)

    lane = lax.broadcasted_iota(jnp.int32, (8, 128), 1)
    sample = STRIDE * (plane * ROWS + core * 64 + (lane & 63)) - IMAGE // 2
    cross_sign = jnp.where(lane < 64, 1.0, -1.0)

    def transform(step, subs):
        to_x = lax.rem(here_x + ORDER[step], 4)
        place = pl.ds(pl.multiple_of(to_x * 256, 256), 256)
        lhs = table[place, :]
        straight, crossed = [None] * 32, [None] * 32
        if subs[0] > 0:
            straight = [sums[step, 0, 8 * i : 8 * i + 8] for i in range(32)]
            crossed = [sums[step, 1, 8 * i : 8 * i + 8] for i in range(32)]
        for sub in subs:
            rhs = jnp.concatenate([weights[sub], incoming[sub]], axis=1)
            product = jnp.dot(lhs, rhs, preferred_element_type=jnp.float32)
            for side in range(2):
                which = OWN * side + sub
                shift_u, shift_v = shift_of(0, which), shift_of(1, which)
                double = advance[which : which + 1]

                def anchor(at):
                    pixel = STRIDE * (to_x * 256 + 8 * at + which_row) - IMAGE // 2
                    turns = (pixel * shift_v + sample * shift_u) & (2 * IMAGE - 1)
                    frac = turns.astype(jnp.float32) * (1.0 / (2 * IMAGE))
                    return cos_turns(frac), cos_turns(frac - 0.25) * cross_sign

                below, above = anchor(15), anchor(16)
                for before, now, order in ((below, above, range(16, 32)), (above, below, range(15, -1, -1))):
                    for at in order:
                        part = product[8 * at : 8 * at + 8, 128 * side : 128 * side + 128]
                        add, cross = part * now[0], part * now[1]
                        straight[at] = add if straight[at] is None else straight[at] + add
                        crossed[at] = cross if crossed[at] is None else crossed[at] + cross
                        after = tuple(double * b - a for a, b in zip(before, now))
                        before, now = now, after
        if subs[-1] < OWN - 1:
            sums[step, 0] = jnp.concatenate(straight, axis=0)
            sums[step, 1] = jnp.concatenate(crossed, axis=0)
            return
        total = jnp.concatenate(straight, axis=0) + pltpu.roll(jnp.concatenate(crossed, axis=0), 64, 1)
        if step == 3:
            kept[...] = total
        blocks[step] = total.astype(jnp.bfloat16)

    early, late = (0, 1, 2), (3,)
    pair_copy(0).wait_recv()
    pair_copy(1).wait_recv()
    for step in range(4):
        transform(step, early)
    pair_copy(2).wait_recv()
    for steps in ((0,), (1,), (2,), (3,)):
        for step in steps:
            transform(step, late)
        for step in steps:
            for hop in hops_of(step):
                block_copy(step, hop).start()

    total = kept[pl.ds(pl.multiple_of(here_y * 64, 64), 64), :]
    for step in range(4):
        for hop in hops_of(step):
            block_copy(step, hop).wait_recv()
    for step in range(4):
        for hop in hops_of(step):
            total = total + slots[step, hop].astype(jnp.float32)
    result[...] = total * window[pl.ds(pl.multiple_of(lax.rem(row, 2) * 64, 64), 64), :]
    for number in range(3):
        pair_copy(number).wait_send()
    for step in range(4):
        for hop in hops_of(step):
            block_copy(step, hop).wait_send()


def per_device(visibility, baseline, offsets, counts, taper_x, taper_y):
    hbm = pl.BlockSpec(memory_space=pltpu.HBM)
    half = jnp.bfloat16
    full = jnp.float32
    total = pl.pallas_call(
        kernel,
        out_shape=jax.ShapeDtypeStruct((64, 128), full),
        in_specs=[hbm] * 7,
        out_specs=pl.BlockSpec(memory_space=pltpu.VMEM),
        scratch_shapes=[
            pltpu.VMEM((OWN, 2, SIDE), full),
            pltpu.VMEM((OWN, 2, SIDE), full),
            pltpu.SMEM((2, 8), jnp.int32),
            pltpu.SMEM((8,), jnp.int32),
            pltpu.VMEM((2, 1, SIDE), full),
            pltpu.VMEM((SIDE, SIDE), half),
            pltpu.VMEM((2 * ROWS, SIDE), half),
            pltpu.VMEM((112, 128), full),
            pltpu.VMEM((40, SIDE), full),
            pltpu.VMEM((8, SIDE, 128), half),
            pltpu.VMEM((8, SIDE, 128), half),
            pltpu.VMEM((2, SIDE, 128), half),
            pltpu.VMEM((OWN, SIDE, 128), half),
            pltpu.VMEM((OWN, SIDE, 128), half),
            pltpu.VMEM((OWN, SIDE, 128), half),
            pltpu.VMEM((8, 128), full),
            pltpu.VMEM((128, 128), full),
            pltpu.VMEM((4, 2, 256, 128), full),
            pltpu.VMEM((256, 128), full),
            pltpu.VMEM((4, 256, 128), half),
            pltpu.VMEM((4, 4, 64, 128), half),
            pltpu.SemaphoreType.DMA((7,)),
            pltpu.SemaphoreType.DMA((3,)),
            pltpu.SemaphoreType.DMA((3,)),
            pltpu.SemaphoreType.DMA((4, 4)),
            pltpu.SemaphoreType.DMA((4, 4)),
        ],
        compiler_params=pltpu.CompilerParams(
            collective_id=0, has_side_effects=True, vmem_limit_bytes=48 * 1024 * 1024
        ),
        name="facet_rows",
    )(
        *(
            pltpu.with_memory_space_constraint(array, pltpu.HBM)
            for array in (
                visibility,
                baseline,
                offsets.T,
                counts,
                taper_x.reshape(1, SIDE),
                taper_y.reshape(1, SIDE),
                jnp.asarray(half_table()),
            )
        )
    )
    return total.T.reshape(2, 64, 64)


def solution(mesh):
    placed = (P("row", None, None), P("row", None, None), P("row", None), P("row"), P(), P())
    return jax.shard_map(
        per_device, mesh=mesh, in_specs=placed, out_specs=P(None, "col", "row"), check_vma=False
    )
```
